256 devices in a mesh: dom: 64 (over z, x, core), rep: 4 (over y).
Axes of the slice: x: 4, y: 4, z: 8, core: 2. Of those that a mesh axis runs over, the one named last changes fastest.
Arguments:
- entities: bfloat16 [65536, 512], P('dom'), may hold values from -60 to 60
- relations: bfloat16 [4, 512, 512], replicated, may hold values from -2 to 2
- head_local: int32 [131072], P(('dom', 'rep')), may hold values from 0 to 1023
- rel_ids: int32 [131072], P(('dom', 'rep')), may hold values from 0 to 3
- tail_part: int32 [131072, 1], P(('dom', 'rep')), may hold values from 0 to 63; in each aligned block of 512 rows (0 to 511, 512 to 1023, ...) at most 16 rows name the same one
- tail_local: int32 [131072], P(('dom', 'rep')), may hold values from 0 to 1023
- neg_local: int32 [2048], P('dom'), may hold values from 0 to 1023
Outputs:
- entity_grad: float32 [65536, 512], P('dom')
- relation_grad: float32 [4, 512, 512], replicated
- edge_loss: float32 [131072], P(('dom', 'rep'))
The draws below stay inside these ranges and needn't reach their ends.
Inputs may be any that keep to these rules, and one draw needn't show every extreme that they name: `tail_part`: in the 512 edges of one device no partition is named by more than 16 edges, a bound that some block reaches.
All inputs are finite; a program needn't handle non-finite values.
Results may differ from the reference program's by a relative error of at most 0.012.
The reference program's roundings to bfloat16 on the way (of `queries`, `prob_neg` and `query_grad`) count: a program that leaves them out, or rounds other values in their place, can miss the bound.
Values may be sent and summed in bfloat16 or wider, within the bound.
A program may use at most 64 MiB of HBM per device.

```python
import math
import jax
import jax.numpy as jnp
import numpy as np
from jax import lax

D = 512
REL = 4
ENT_DEV = 1024
E_DEV = 512
NEG_DEV = 32
ENT = 65536
EDGES = 131072
NEG = 2048
CAP = 16
N_DOM = 64
N_REP = 4


def draw_entities(key, part):
    first = jax.random.fold_in(key, 0)
    values = jnp.clip(jax.random.normal(first, (ENT_DEV * N_DOM, D), jnp.float32), -6.0, 6.0)
    return values.astype(jnp.bfloat16)


def draw_relations(key, part):
    first, second = jax.random.split(key)
    spread = 0.8 / math.sqrt(D)
    noise = jnp.clip(jax.random.normal(first, (REL, D, D), jnp.float32), -4.0, 4.0) * spread
    diagonal = jax.random.uniform(second, (REL, 1, 1), jnp.float32, 0.6, 1.4)
    identity = (jnp.arange(D)[:, None] == jnp.arange(D)[None, :]).astype(jnp.float32)
    return (diagonal * identity + noise).astype(jnp.bfloat16)


def touch_ends(values, own_key, smallest, top_value):
    extent = values.shape
    place = [jax.random.randint(jax.random.fold_in(own_key, axis), (), 0, extent[axis]) for axis in range(len(extent))]
    values = values.at[tuple(place)].set(smallest)
    longest = extent.index(max(extent))
    place[longest] = (place[longest] + 1) % extent[longest]
    return values.at[tuple(place)].set(top_value)


def deal_out(rng, own, number, rows, number_of, top, limit, slope):
    sequence = jax.random.permutation(rng, number_of)
    crowded, common = portions_of(number_of, rows * top, limit, slope, True), portions_of(number_of, rows * top, limit, slope, False)
    places = jnp.arange(number_of)

    def named(sizes, offset_by):
        used = int((sizes > 0).sum())
        fixed = max(1, used // 4)
        moved = fixed + (places - fixed + offset_by * (used - fixed)) % max(1, number_of - fixed)
        return jnp.zeros((number_of,), jnp.int32).at[sequence[jnp.where(places < fixed, places, moved)]].set(jnp.asarray(sizes, jnp.int32))

    sizes = jnp.where(number % 4 == 0, named(crowded, number // 4), named(common, number - number // 4 - 1))
    mixed = jax.random.permutation(jax.random.fold_in(own, 3), number_of)
    giver, sink = mixed[0:number_of // 2 * 2:2], mixed[1:number_of // 2 * 2:2]
    slack = jnp.minimum(sizes[giver] - 1, limit - sizes[sink]) // 2
    slack = jnp.where((giver == sequence[0]) | (sink == sequence[0]) | (sizes[sink] == 0), 0, jnp.maximum(slack, 0))
    moved = jax.random.randint(jax.random.fold_in(own, 4), (number_of // 2,), 0, 1 << 20) % (slack + 1)
    sizes = sizes.at[giver].add(-moved).at[sink].add(moved)
    items = jnp.searchsorted(jnp.cumsum(sizes), jnp.arange(rows * top), side="right").astype(jnp.int32)
    table = items.reshape(top, rows).T
    table = table[jax.random.permutation(jax.random.fold_in(own, 1), rows)]
    offset_by = jax.random.randint(jax.random.fold_in(own, 2), (rows, 1), 0, top)
    return jnp.take_along_axis(table, (jnp.arange(top)[None, :] + offset_by) % top, axis=1)


def portions_of(number_of, total, bound, lean, full):
    portions = [(1 << 20) // math.isqrt(grade ** lean) + 1 for grade in range(1, number_of + 1)]
    largest = bound if full else min(bound, max(-(-total // number_of), total * portions[0] // sum(portions)))
    least = 1 if total - largest >= number_of - 1 else 0
    holding, surplus = [largest] + [least] * (number_of - 1), total - largest - least * (number_of - 1)
    while surplus > 0:
        free = [i for i in range(1, number_of) if holding[i] < largest] or [i for i in range(1, number_of) if holding[i] < bound]
        whole, remaining = sum([portions[i] for i in free]), surplus
        for i in free:
            extra = min(bound - holding[i], max(1, remaining * portions[i] // whole), surplus)
            holding[i] = holding[i] + extra
            surplus = surplus - extra
    return np.array(holding)


def setup_inputs(seed: int = 0) -> dict:
    streams_of = jax.random.split(jax.random.key(seed), 8)
    entities = draw_entities(jax.random.fold_in(streams_of[7], 71), 0)
    relations = draw_relations(jax.random.fold_in(streams_of[7], 71), 0)
    head_local = touch_ends(jax.random.randint(streams_of[2], (EDGES,), 0, ENT_DEV), jax.random.fold_in(streams_of[2], 1), 0, ENT_DEV - 1).astype(jnp.int32)
    rel_ids = touch_ends(jax.random.randint(streams_of[3], (EDGES,), 0, REL), jax.random.fold_in(streams_of[3], 1), 0, REL - 1).astype(jnp.int32)
    tail_part_keys = jax.random.split(jax.random.fold_in(streams_of[4], 1), EDGES // E_DEV)
    tail_part_turns = jax.random.permutation(jax.random.fold_in(streams_of[4], 3), EDGES // E_DEV)
    tail_part = jax.vmap(lambda own, number: deal_out(jax.random.fold_in(streams_of[4], 2), own, number, E_DEV, N_DOM, 1, CAP, 2))(tail_part_keys, tail_part_turns).reshape((EDGES, 1))
    tail_local = touch_ends(jax.random.randint(streams_of[5], (EDGES,), 0, ENT_DEV), jax.random.fold_in(streams_of[5], 1), 0, ENT_DEV - 1).astype(jnp.int32)
    neg_local = touch_ends(jax.random.randint(streams_of[6], (NEG,), 0, ENT_DEV), jax.random.fold_in(streams_of[6], 1), 0, ENT_DEV - 1).astype(jnp.int32)
    return dict(entities=entities, relations=relations, head_local=head_local, rel_ids=rel_ids, tail_part=tail_part, tail_local=tail_local, neg_local=neg_local)


def edge_block(queries, tail_embed, negatives, factor):
    positive = lax.optimization_barrier(jnp.sum(queries.astype(jnp.float32) * tail_embed.astype(jnp.float32), axis=1)) * factor
    scores = lax.dot_general(queries, negatives, (((1,), (1,)), ((), ())), preferred_element_type=jnp.float32) * factor
    row_max = jnp.maximum(positive, lax.optimization_barrier(jnp.max(scores, axis=1)))
    exp_pos = jnp.exp(positive - row_max)
    exp_neg = jnp.exp(scores - row_max[:, None])
    partition_sum = exp_pos + lax.optimization_barrier(jnp.sum(exp_neg, axis=1))
    edge_loss = jnp.log(partition_sum) + row_max - positive
    prob_pos = exp_pos / partition_sum
    prob_neg = (exp_neg / partition_sum[:, None]).astype(jnp.bfloat16)
    mixed = jnp.dot(prob_neg, negatives, preferred_element_type=jnp.float32)
    query_grad = (factor * ((prob_pos - 1.0)[:, None] * tail_embed.astype(jnp.float32) + mixed)).astype(jnp.bfloat16)
    tail_grad = factor * (prob_pos - 1.0)[:, None] * queries.astype(jnp.float32)
    neg_grad = factor * lax.dot_general(prob_neg, queries, (((0,), (0,)), ((), ())), preferred_element_type=jnp.float32)
    return (edge_loss, query_grad, tail_grad, neg_grad)

def reference(entities, relations, head_local, rel_ids, tail_part, tail_local, neg_local):
    factor = 1.0 / math.sqrt(D)
    neg_ids = jnp.arange(NEG, dtype=jnp.int32) // NEG_DEV * ENT_DEV + neg_local
    negatives = jnp.take(entities, neg_ids, axis=0)
    blocks = EDGES // E_DEV

    def one_block(carry, block):
        entity_acc, relation_acc, negative_acc = carry
        start = (block * E_DEV).astype(jnp.int32)
        owner = (block // N_REP).astype(jnp.int32)
        head_ids = owner * ENT_DEV + lax.dynamic_slice_in_dim(head_local, start, E_DEV)
        rel_block = lax.dynamic_slice_in_dim(rel_ids, start, E_DEV)
        tail_ids = lax.dynamic_slice_in_dim(tail_part[:, 0], start, E_DEV) * ENT_DEV + lax.dynamic_slice_in_dim(tail_local, start, E_DEV)
        head_rows = jnp.take(entities, head_ids, axis=0)
        tail_embed = jnp.take(entities, tail_ids, axis=0)
        query_sum = jnp.zeros((E_DEV, D), jnp.float32)
        for relation in range(REL):
            picked = jnp.where((rel_block == relation)[:, None], head_rows, jnp.zeros_like(head_rows))
            query_sum = query_sum + jnp.dot(picked, relations[relation], preferred_element_type=jnp.float32)
        queries = query_sum.astype(jnp.bfloat16)
        edge_loss, query_grad, tail_grad, neg_grad = edge_block(queries, tail_embed, negatives, factor)
        head_grad = jnp.zeros((E_DEV, D), jnp.float32)
        rel_terms = []
        for relation in range(REL):
            selector = (rel_block == relation)[:, None]
            picked_grad = jnp.where(selector, query_grad, jnp.zeros_like(query_grad))
            head_grad = head_grad + lax.dot_general(picked_grad, relations[relation], (((1,), (1,)), ((), ())), preferred_element_type=jnp.float32)
            picked_rows = jnp.where(selector, head_rows, jnp.zeros_like(head_rows))
            rel_terms.append(lax.dot_general(picked_rows, query_grad, (((0,), (0,)), ((), ())), preferred_element_type=jnp.float32))
        entity_acc = entity_acc.at[head_ids].add(head_grad).at[tail_ids].add(tail_grad)
        relation_acc = relation_acc + jnp.stack(rel_terms)
        negative_acc = negative_acc + neg_grad
        return ((entity_acc, relation_acc, negative_acc), edge_loss)
    initial = (jnp.zeros((ENT, D), jnp.float32), jnp.zeros((REL, D, D), jnp.float32), jnp.zeros((NEG, D), jnp.float32))
    (entity_acc, relation_acc, negative_acc), losses = lax.scan(one_block, initial, jnp.arange(blocks, dtype=jnp.int32))
    entity_acc = entity_acc.at[neg_ids].add(negative_acc)
    return (entity_acc, relation_acc, losses.reshape(EDGES))
```

```python
import functools
import math

import jax
import jax.numpy as jnp
from jax import lax
from jax.experimental import pallas as pl
from jax.experimental.pallas import tpu as pltpu
from jax.sharding import PartitionSpec as P

D = 512


def _stage(name, dom, rep, n_dom, n_rep):
    core, xx, zz = dom % 2, (dom // 2) % 4, dom // 8
    if name == "core":
        return 2, core, lambda j: ((zz * 4 + xx) * 2 + j, rep)
    if name == "x":
        return min(4, n_dom // 2), xx, lambda j: ((zz * 4 + j) * 2 + core, rep)
    if name == "y":
        return n_rep, rep, lambda j: (dom, j)
    return max(1, n_dom // 8), zz, lambda j: ((j * 4 + xx) * 2 + core, rep)


def _sum_rows(parts, dst, rows):
    step = min(rows, 64)

    def body(i, carry):
        at = pl.ds(pl.multiple_of(i * step, 8), step)
        total = parts[0](at)
        for part in parts[1:]:
            total = total + part(at)
        dst[at, :] = total
        return carry

    lax.fori_loop(0, rows // step, body, 0)


def _reduce_kernel(rs, ag, sizes, x_ref, out_ref, *scratch):
    n_dom, n_rep = sizes
    dom = lax.axis_index("dom")
    rep = lax.axis_index("rep")
    mesh_id = pl.DeviceIdType.MESH
    rs_info = [_stage(n, dom, rep, n_dom, n_rep) for n in rs]
    ag_info = [_stage(n, dom, rep, n_dom, n_rep) for n in ag]
    nr = len(rs)
    recv_bufs = scratch[:nr]
    acc_bufs = scratch[nr : 2 * nr]
    full = scratch[2 * nr]
    rs_send, rs_recv, ag_send, ag_recv = scratch[2 * nr + 1 : 2 * nr + 5]

    barrier = pltpu.get_barrier_semaphore()
    greeted = 0
    seen = set()
    for name, (g, c, peer) in zip(list(rs) + list(ag), rs_info + ag_info):
        if name in seen:
            continue
        seen.add(name)
        for k in range(1, g):
            pl.semaphore_signal(barrier, 1, device_id=peer((c + k) % g), device_id_type=mesh_id)
            greeted += 1
    pl.semaphore_wait(barrier, greeted)

    sends = []
    src = x_ref
    length = x_ref.shape[0]
    base = 0
    si = 0
    for s, (g, c, peer) in enumerate(rs_info):
        piece = length // g
        for k in range(1, g):
            j = (c + k) % g
            cp = pltpu.make_async_remote_copy(
                src_ref=src.at[pl.ds(pl.multiple_of(j * piece, 8), piece)],
                dst_ref=recv_bufs[s].at[g - k - 1],
                send_sem=rs_send.at[si + k - 1],
                recv_sem=rs_recv.at[si + g - k - 1],
                device_id=peer(j),
                device_id_type=mesh_id,
            )
            cp.start()
            sends.append(cp)
        for k in range(1, g):
            j = (c + k) % g
            pltpu.make_async_remote_copy(
                src_ref=src.at[pl.ds(0, piece)],
                dst_ref=recv_bufs[s].at[k - 1],
                send_sem=rs_send.at[si + k - 1],
                recv_sem=rs_recv.at[si + k - 1],
                device_id=peer(j),
                device_id_type=mesh_id,
            ).wait_recv()
        own = pl.multiple_of(c * piece, 8)
        parts = [lambda at, src=src, own=own: src[pl.ds(own + at.start, at.size), :]]
        for k in range(1, g):
            parts.append(lambda at, b=recv_bufs[s], k=k: b[k - 1, at, :])
        _sum_rows(parts, acc_bufs[s], piece)
        src = acc_bufs[s]
        base = base + c * piece
        length = piece
        si += g - 1

    if not ag_info:
        out_ref[...] = src[...]
    else:
        full[pl.ds(pl.multiple_of(base, 8), length), :] = src[...]
        ai = 0
        for g, c, peer in ag_info:
            mine = pl.ds(pl.multiple_of(base, 8), length)
            for k in range(1, g):
                j = (c + k) % g
                cp = pltpu.make_async_remote_copy(
                    src_ref=full.at[mine],
                    dst_ref=full.at[mine],
                    send_sem=ag_send.at[ai + k - 1],
                    recv_sem=ag_recv.at[ai + g - k - 1],
                    device_id=peer(j),
                    device_id_type=mesh_id,
                )
                cp.start()
                sends.append(cp)
            start = base - c * length
            for k in range(1, g):
                j = (c + k) % g
                theirs = pl.ds(pl.multiple_of(start + j * length, 8), length)
                pltpu.make_async_remote_copy(
                    src_ref=full.at[theirs],
                    dst_ref=full.at[theirs],
                    send_sem=ag_send.at[ai + k - 1],
                    recv_sem=ag_recv.at[ai + k - 1],
                    device_id=peer(j),
                    device_id_type=mesh_id,
                ).wait_recv()
            base = start
            length = length * g
            ai += g - 1
        out_ref[...] = full[...]
    for cp in sends:
        cp.wait_send()


def tree_reduce(x, rs, ag, collective_id):
    n_dom = lax.axis_size("dom")
    n_rep = lax.axis_size("rep")
    rows, columns = x.shape
    shapes = []
    length = rows
    rs_sizes = []
    for name in rs:
        g = _stage(name, 0, 0, n_dom, n_rep)[0]
        rs_sizes.append(g)
    accs = []
    for g in rs_sizes:
        piece = length // g
        shapes.append(pltpu.VMEM((max(g - 1, 1), piece, columns), jnp.float32))
        accs.append(pltpu.VMEM((piece, columns), jnp.float32))
        length = piece
    n_ag = sum(_stage(name, 0, 0, n_dom, n_rep)[0] - 1 for name in ag)
    out_rows = rows if ag else length
    scratch = shapes + accs + [
        pltpu.VMEM((rows if ag else 8, columns), jnp.float32),
        pltpu.SemaphoreType.DMA((max(1, sum(g - 1 for g in rs_sizes)),)),
        pltpu.SemaphoreType.DMA((max(1, sum(g - 1 for g in rs_sizes)),)),
        pltpu.SemaphoreType.DMA((max(1, n_ag),)),
        pltpu.SemaphoreType.DMA((max(1, n_ag),)),
    ]
    return pl.pallas_call(
        functools.partial(_reduce_kernel, tuple(rs), tuple(ag), (n_dom, n_rep)),
        out_shape=jax.ShapeDtypeStruct((out_rows, columns), jnp.float32),
        in_specs=[pl.BlockSpec(memory_space=pltpu.VMEM)],
        out_specs=pl.BlockSpec(memory_space=pltpu.VMEM),
        scratch_shapes=scratch,
        compiler_params=pltpu.CompilerParams(
            collective_id=collective_id, has_side_effects=True, vmem_limit_bytes=60 * 1024 * 1024
        ),
        cost_estimate=pl.CostEstimate(
            flops=rows * columns * 2, transcendentals=0, bytes_accessed=rows * columns * 16
        ),
    )(x)


def local(entities, relations, head_local, rel_ids, tail_part, tail_local, neg_local):
    factor = 1.0 / math.sqrt(D)
    ent_dev = entities.shape[0]
    columns = entities.shape[1]
    edge_count = head_local.shape[0]
    part_count = lax.axis_size("dom")
    capacity = 2 * edge_count // part_count
    slot_count = part_count * capacity
    relation_count = relations.shape[0]
    head_rows = jnp.take(entities, head_local, axis=0)
    selectors = [(rel_ids == relation)[:, None] for relation in range(relation_count)]
    query_sum = jnp.zeros((edge_count, columns), jnp.float32)
    for relation in range(relation_count):
        picked = jnp.where(selectors[relation], head_rows, jnp.zeros_like(head_rows))
        query_sum = query_sum + jnp.dot(
            picked, relations[relation], preferred_element_type=jnp.float32
        )
    queries = query_sum.astype(jnp.bfloat16)
    target = tail_part[:, 0]
    target_hot = (target[:, None] == jnp.arange(part_count, dtype=jnp.int32)[None, :]).astype(
        jnp.int32
    )
    earlier = jnp.cumsum(target_hot, axis=0) - target_hot
    position = jnp.sum(earlier * target_hot, axis=1)
    slot_index = target * capacity + position
    slot_match = (slot_index[None, :] == jnp.arange(slot_count, dtype=jnp.int32)[:, None]).astype(
        jnp.int32
    )
    filled = jnp.sum(slot_match, axis=1) > 0
    source = jnp.sum(slot_match * jnp.arange(edge_count, dtype=jnp.int32)[None, :], axis=1)
    send_ids = jnp.where(filled, jnp.take(tail_local, source, axis=0), 0).reshape(
        part_count, capacity
    )
    recv_ids = lax.all_to_all(send_ids, "dom", split_axis=0, concat_axis=0, tiled=True)
    looked_up = jnp.take(entities, recv_ids.reshape(-1), axis=0).reshape(
        part_count, capacity, columns
    )
    returned = lax.all_to_all(looked_up, "dom", split_axis=0, concat_axis=0, tiled=True)
    tail_embed = jnp.take(returned.reshape(slot_count, columns), slot_index, axis=0)
    own_negs = jnp.take(entities, neg_local, axis=0)
    negatives = lax.all_gather(own_negs, "dom", axis=0, tiled=True)
    positive = (
        jnp.sum(queries.astype(jnp.float32) * tail_embed.astype(jnp.float32), axis=1) * factor
    )
    scores = (
        lax.dot_general(
            queries, negatives, (((1,), (1,)), ((), ())), preferred_element_type=jnp.float32
        )
        * factor
    )
    row_max = jnp.maximum(positive, jnp.max(scores, axis=1))
    exp_pos = jnp.exp(positive - row_max)
    exp_neg = jnp.exp(scores - row_max[:, None])
    partition_sum = exp_pos + jnp.sum(exp_neg, axis=1)
    edge_loss = jnp.log(partition_sum) + row_max - positive
    prob_pos = exp_pos / partition_sum
    prob_neg = (exp_neg / partition_sum[:, None]).astype(jnp.bfloat16)
    mixed = jnp.dot(prob_neg, negatives, preferred_element_type=jnp.float32)
    query_grad = (
        factor * ((prob_pos - 1.0)[:, None] * tail_embed.astype(jnp.float32) + mixed)
    ).astype(jnp.bfloat16)
    tail_grad = factor * (prob_pos - 1.0)[:, None] * queries.astype(jnp.float32)
    head_grad = jnp.zeros((edge_count, columns), jnp.float32)
    rel_terms = []
    for relation in range(relation_count):
        picked_grad = jnp.where(selectors[relation], query_grad, jnp.zeros_like(query_grad))
        head_grad = head_grad + lax.dot_general(
            picked_grad,
            relations[relation],
            (((1,), (1,)), ((), ())),
            preferred_element_type=jnp.float32,
        )
        picked_rows = jnp.where(selectors[relation], head_rows, jnp.zeros_like(head_rows))
        rel_terms.append(
            lax.dot_general(
                picked_rows,
                query_grad,
                (((0,), (0,)), ((), ())),
                preferred_element_type=jnp.float32,
            )
        )
    rel_stack, prob_neg_late, queries_late = lax.optimization_barrier(
        (jnp.stack(rel_terms), prob_neg, queries)
    )
    relation_grad = tree_reduce(
        rel_stack.reshape(-1, columns), ("core", "x", "y", "z"), ("z", "y", "x", "core"), 0
    ).reshape(rel_stack.shape)
    neg_grad = factor * lax.dot_general(
        prob_neg_late, queries_late, (((0,), (0,)), ((), ())), preferred_element_type=jnp.float32
    )
    grad_send = jnp.where(filled[:, None], jnp.take(tail_grad, source, axis=0), 0.0)
    grad_recv = lax.all_to_all(
        grad_send.reshape(part_count, capacity, columns),
        "dom",
        split_axis=0,
        concat_axis=0,
        tiled=True,
    )
    neg_parts = lax.all_to_all(
        neg_grad.reshape(part_count, -1, columns), "dom", split_axis=0, concat_axis=0, tiled=True
    )
    owned = jnp.sum(neg_parts, axis=0)
    target_ids = jnp.concatenate([head_local, recv_ids.reshape(-1), neg_local])
    target_rows = jnp.concatenate(
        [head_grad, grad_recv.reshape(slot_count, columns), owned], axis=0
    )
    block_rows = min(512, ent_dev)
    block_count = ent_dev // block_rows

    def add_block(start):
        hot = (
            target_ids[None, :] == (start + jnp.arange(block_rows, dtype=jnp.int32))[:, None]
        ).astype(jnp.float32)
        return jnp.dot(
            hot, target_rows, precision=lax.Precision.HIGHEST, preferred_element_type=jnp.float32
        )

    local_grad = lax.map(add_block, jnp.arange(block_count, dtype=jnp.int32) * block_rows).reshape(
        ent_dev, columns
    )
    entity_grad = lax.psum(local_grad, "rep")
    return (entity_grad, relation_grad, edge_loss)


def solution(mesh):
    return jax.shard_map(
        local,
        mesh=mesh,
        in_specs=(
            P("dom", None),
            P(),
            P(("dom", "rep")),
            P(("dom", "rep")),
            P(("dom", "rep"), None),
            P(("dom", "rep")),
            P("dom"),
        ),
        out_specs=(P("dom", None), P(), P(("dom", "rep"))),
        check_vma=False,
    )
```

```python
import functools
import math

import jax
import jax.numpy as jnp
from jax import lax
from jax.experimental import pallas as pl
from jax.experimental.pallas import tpu as pltpu
from jax.sharding import PartitionSpec as P

D = 512


def _stage(name, dom, rep, n_dom, n_rep):
    core, xx, zz = dom % 2, (dom // 2) % 4, dom // 8
    if name == "core":
        return 2, core, lambda j: ((zz * 4 + xx) * 2 + j, rep)
    if name == "x":
        return min(4, n_dom // 2), xx, lambda j: ((zz * 4 + j) * 2 + core, rep)
    if name == "y":
        return n_rep, rep, lambda j: (dom, j)
    return max(1, n_dom // 8), zz, lambda j: ((j * 4 + xx) * 2 + core, rep)


def _sum_rows(parts, dst, rows):
    step = min(rows, 64)

    def body(i, carry):
        at = pl.ds(pl.multiple_of(i * step, 8), step)
        total = parts[0](at)
        for part in parts[1:]:
            total = total + part(at)
        dst[at, :] = total
        return carry

    lax.fori_loop(0, rows // step, body, 0)


def _reduce_kernel(rs, ag, sizes, x_ref, out_ref, *scratch):
    n_dom, n_rep = sizes
    dom = lax.axis_index("dom")
    rep = lax.axis_index("rep")
    mesh_id = pl.DeviceIdType.MESH
    rs_info = [_stage(n, dom, rep, n_dom, n_rep) for n in rs]
    ag_info = [_stage(n, dom, rep, n_dom, n_rep) for n in ag]
    nr = len(rs)
    recv_bufs = scratch[:nr]
    acc_bufs = scratch[nr : 2 * nr]
    full = scratch[2 * nr]
    rs_send, rs_recv, ag_send, ag_recv = scratch[2 * nr + 1 : 2 * nr + 5]

    barrier = pltpu.get_barrier_semaphore()
    greeted = 0
    seen = set()
    for name, (g, c, peer) in zip(list(rs) + list(ag), rs_info + ag_info):
        if name in seen:
            continue
        seen.add(name)
        for k in range(1, g):
            pl.semaphore_signal(barrier, 1, device_id=peer((c + k) % g), device_id_type=mesh_id)
            greeted += 1
    pl.semaphore_wait(barrier, greeted)

    sends = []
    src = x_ref
    length = x_ref.shape[0]
    base = 0
    si = 0
    for s, (g, c, peer) in enumerate(rs_info):
        piece = length // g
        for k in range(1, g):
            j = (c + k) % g
            cp = pltpu.make_async_remote_copy(
                src_ref=src.at[pl.ds(pl.multiple_of(j * piece, 8), piece)],
                dst_ref=recv_bufs[s].at[g - k - 1],
                send_sem=rs_send.at[si + k - 1],
                recv_sem=rs_recv.at[si + g - k - 1],
                device_id=peer(j),
                device_id_type=mesh_id,
            )
            cp.start()
            sends.append(cp)
        for k in range(1, g):
            j = (c + k) % g
            pltpu.make_async_remote_copy(
                src_ref=src.at[pl.ds(0, piece)],
                dst_ref=recv_bufs[s].at[k - 1],
                send_sem=rs_send.at[si + k - 1],
                recv_sem=rs_recv.at[si + k - 1],
                device_id=peer(j),
                device_id_type=mesh_id,
            ).wait_recv()
        own = pl.multiple_of(c * piece, 8)
        parts = [lambda at, src=src, own=own: src[pl.ds(own + at.start, at.size), :]]
        for k in range(1, g):
            parts.append(lambda at, b=recv_bufs[s], k=k: b[k - 1, at, :])
        _sum_rows(parts, acc_bufs[s], piece)
        src = acc_bufs[s]
        base = base + c * piece
        length = piece
        si += g - 1

    if not ag_info:
        out_ref[...] = src[...]
    else:
        full[pl.ds(pl.multiple_of(base, 8), length), :] = src[...]
        ai = 0
        for g, c, peer in ag_info:
            mine = pl.ds(pl.multiple_of(base, 8), length)
            for k in range(1, g):
                j = (c + k) % g
                cp = pltpu.make_async_remote_copy(
                    src_ref=full.at[mine],
                    dst_ref=full.at[mine],
                    send_sem=ag_send.at[ai + k - 1],
                    recv_sem=ag_recv.at[ai + g - k - 1],
                    device_id=peer(j),
                    device_id_type=mesh_id,
                )
                cp.start()
                sends.append(cp)
            start = base - c * length
            for k in range(1, g):
                j = (c + k) % g
                theirs = pl.ds(pl.multiple_of(start + j * length, 8), length)
                pltpu.make_async_remote_copy(
                    src_ref=full.at[theirs],
                    dst_ref=full.at[theirs],
                    send_sem=ag_send.at[ai + k - 1],
                    recv_sem=ag_recv.at[ai + k - 1],
                    device_id=peer(j),
                    device_id_type=mesh_id,
                ).wait_recv()
            base = start
            length = length * g
            ai += g - 1
        out_ref[...] = full[...]
    for cp in sends:
        cp.wait_send()


def tree_reduce(x, rs, ag, collective_id):
    n_dom = lax.axis_size("dom")
    n_rep = lax.axis_size("rep")
    rows, columns = x.shape
    shapes = []
    length = rows
    rs_sizes = []
    for name in rs:
        g = _stage(name, 0, 0, n_dom, n_rep)[0]
        rs_sizes.append(g)
    accs = []
    for g in rs_sizes:
        piece = length // g
        shapes.append(pltpu.VMEM((max(g - 1, 1), piece, columns), jnp.float32))
        accs.append(pltpu.VMEM((piece, columns), jnp.float32))
        length = piece
    n_ag = sum(_stage(name, 0, 0, n_dom, n_rep)[0] - 1 for name in ag)
    out_rows = rows if ag else length
    scratch = shapes + accs + [
        pltpu.VMEM((rows if ag else 8, columns), jnp.float32),
        pltpu.SemaphoreType.DMA((max(1, sum(g - 1 for g in rs_sizes)),)),
        pltpu.SemaphoreType.DMA((max(1, sum(g - 1 for g in rs_sizes)),)),
        pltpu.SemaphoreType.DMA((max(1, n_ag),)),
        pltpu.SemaphoreType.DMA((max(1, n_ag),)),
    ]
    return pl.pallas_call(
        functools.partial(_reduce_kernel, tuple(rs), tuple(ag), (n_dom, n_rep)),
        out_shape=jax.ShapeDtypeStruct((out_rows, columns), jnp.float32),
        in_specs=[pl.BlockSpec(memory_space=pltpu.VMEM)],
        out_specs=pl.BlockSpec(memory_space=pltpu.VMEM),
        scratch_shapes=scratch,
        compiler_params=pltpu.CompilerParams(
            collective_id=collective_id, has_side_effects=True, vmem_limit_bytes=60 * 1024 * 1024
        ),
        cost_estimate=pl.CostEstimate(
            flops=rows * columns * 2, transcendentals=0, bytes_accessed=rows * columns * 16
        ),
    )(x)


def _lane_kernel(lanes, sizes, n_in, *refs):
    n_dom, n_rep = sizes
    ins = refs[:n_in]
    outs = refs[n_in : 2 * n_in]
    scratch = refs[2 * n_in :]
    dom = lax.axis_index("dom")
    rep = lax.axis_index("rep")
    mesh_id = pl.DeviceIdType.MESH
    pos = 0
    lane_bufs = []
    for _, _, _, rs, _ in lanes:
        lane_bufs.append((scratch[pos : pos + len(rs)], scratch[pos + len(rs) : pos + 2 * len(rs)]))
        pos += 2 * len(rs)
    fulls = scratch[pos : pos + n_in]
    rs_send, rs_recv, ag_send, ag_recv = scratch[pos + n_in : pos + n_in + 4]

    def info(name):
        return _stage(name, dom, rep, n_dom, n_rep)

    barrier = pltpu.get_barrier_semaphore()
    greeted = 0
    names = []
    for lane in lanes:
        for name in lane[3] + lane[4]:
            if name not in names:
                names.append(name)
    for name in names:
        g, c, peer = info(name)
        for k in range(1, g):
            pl.semaphore_signal(barrier, 1, device_id=peer((c + k) % g), device_id_type=mesh_id)
            greeted += 1
    pl.semaphore_wait(barrier, greeted)

    sends = []
    state = [
        (ins[i], c0, w, ins[i].shape[0], 0) for i, c0, w, _, _ in lanes
    ]
    rs_base = []
    total = 0
    for lane in lanes:
        rs_base.append(total)
        total += sum(info(name)[0] - 1 for name in lane[3])
    for t in range(max(len(lane[3]) for lane in lanes)):
        pending = []
        offsets = [rs_base[li] + sum(info(n)[0] - 1 for n in lane[3][:t]) for li, lane in enumerate(lanes)]
        for li, lane in enumerate(lanes):
            if t >= len(lane[3]):
                continue
            g, c, peer = info(lane[3][t])
            ref, c0, w, length, gbase = state[li]
            piece = length // g
            si = offsets[li]
            recv = lane_bufs[li][0][t]
            for k in range(1, g):
                j = (c + k) % g
                cp = pltpu.make_async_remote_copy(
                    src_ref=ref.at[pl.ds(pl.multiple_of(j * piece, 8), piece), pl.ds(c0, w)],
                    dst_ref=recv.at[g - k - 1],
                    send_sem=rs_send.at[si + k - 1],
                    recv_sem=rs_recv.at[si + g - k - 1],
                    device_id=peer(j),
                    device_id_type=mesh_id,
                )
                cp.start()
                sends.append(cp)
            pending.append(li)
        for li in pending:
            lane = lanes[li]
            g, c, peer = info(lane[3][t])
            ref, c0, w, length, gbase = state[li]
            piece = length // g
            si = offsets[li]
            recv = lane_bufs[li][0][t]
            acc = lane_bufs[li][1][t]
            for k in range(1, g):
                j = (c + k) % g
                pltpu.make_async_remote_copy(
                    src_ref=ref.at[pl.ds(0, piece), pl.ds(c0, w)],
                    dst_ref=recv.at[k - 1],
                    send_sem=rs_send.at[si + k - 1],
                    recv_sem=rs_recv.at[si + k - 1],
                    device_id=peer(j),
                    device_id_type=mesh_id,
                ).wait_recv()
            own = pl.multiple_of(c * piece, 8)
            parts = [lambda at, ref=ref, own=own, c0=c0, w=w: ref[pl.ds(own + at.start, at.size), pl.ds(c0, w)]]
            for k in range(1, g):
                parts.append(lambda at, b=recv, k=k: b[k - 1, at, :])
            _sum_rows(parts, acc, piece)
            state[li] = (acc, 0, w, piece, gbase + c * piece)

    ag_state = []
    for li, lane in enumerate(lanes):
        acc, _, w, length, gbase = state[li]
        i, c0 = lane[0], lane[1]
        if lane[4]:
            fulls[i][pl.ds(pl.multiple_of(gbase, 8), length), pl.ds(c0, w)] = acc[...]
        else:
            outs[i][...] = acc[...]
        ag_state.append((length, gbase))
    ag_base = []
    total = 0
    for lane in lanes:
        ag_base.append(total)
        total += sum(info(name)[0] - 1 for name in lane[4])
    for t in range(max(len(lane[4]) for lane in lanes)):
        pending = []
        offsets = [ag_base[li] + sum(info(n)[0] - 1 for n in lane[4][:t]) for li, lane in enumerate(lanes)]
        for li, lane in enumerate(lanes):
            if t >= len(lane[4]):
                continue
            g, c, peer = info(lane[4][t])
            length, gbase = ag_state[li]
            full = fulls[lane[0]]
            cols = pl.ds(lane[1], lane[2])
            mine = pl.ds(pl.multiple_of(gbase, 8), length)
            ai = offsets[li]
            for k in range(1, g):
                j = (c + k) % g
                cp = pltpu.make_async_remote_copy(
                    src_ref=full.at[mine, cols],
                    dst_ref=full.at[mine, cols],
                    send_sem=ag_send.at[ai + k - 1],
                    recv_sem=ag_recv.at[ai + g - k - 1],
                    device_id=peer(j),
                    device_id_type=mesh_id,
                )
                cp.start()
                sends.append(cp)
            pending.append(li)
        for li in pending:
            lane = lanes[li]
            g, c, peer = info(lane[4][t])
            length, gbase = ag_state[li]
            full = fulls[lane[0]]
            cols = pl.ds(lane[1], lane[2])
            ai = offsets[li]
            start = gbase - c * length
            for k in range(1, g):
                j = (c + k) % g
                theirs = pl.ds(pl.multiple_of(start + j * length, 8), length)
                pltpu.make_async_remote_copy(
                    src_ref=full.at[theirs, cols],
                    dst_ref=full.at[theirs, cols],
                    send_sem=ag_send.at[ai + k - 1],
                    recv_sem=ag_recv.at[ai + k - 1],
                    device_id=peer(j),
                    device_id_type=mesh_id,
                ).wait_recv()
            ag_state[li] = (length * g, start)
    gathered = sorted({lane[0] for lane in lanes if lane[4]})
    for i in gathered:
        outs[i][...] = fulls[i][...]
    for cp in sends:
        cp.wait_send()


def lane_reduce(inputs, lanes, collective_id):
    n_dom = lax.axis_size("dom")
    n_rep = lax.axis_size("rep")
    scratch = []
    recv_shapes, acc_shapes = [], []
    n_rs = n_ag = 0
    out_shapes = [None] * len(inputs)
    for i, c0, w, rs, ag in lanes:
        length = inputs[i].shape[0]
        recv, accs = [], []
        for name in rs:
            g = _stage(name, 0, 0, n_dom, n_rep)[0]
            piece = length // g
            recv.append(pltpu.VMEM((max(g - 1, 1), piece, w), jnp.float32))
            accs.append(pltpu.VMEM((piece, w), jnp.float32))
            length = piece
            n_rs += g - 1
        n_ag += sum(_stage(name, 0, 0, n_dom, n_rep)[0] - 1 for name in ag)
        scratch += recv + accs
        out_shapes[i] = inputs[i].shape if ag else (length, w)
    for i, x in enumerate(inputs):
        scratch.append(pltpu.VMEM(x.shape if any(l[0] == i and l[4] for l in lanes) else (8, 128), jnp.float32))
    scratch += [
        pltpu.SemaphoreType.DMA((max(1, n_rs),)),
        pltpu.SemaphoreType.DMA((max(1, n_rs),)),
        pltpu.SemaphoreType.DMA((max(1, n_ag),)),
        pltpu.SemaphoreType.DMA((max(1, n_ag),)),
    ]
    moved = sum(x.size for x in inputs) * 4
    return pl.pallas_call(
        functools.partial(_lane_kernel, tuple(lanes), (n_dom, n_rep), len(inputs)),
        out_shape=[jax.ShapeDtypeStruct(shape, jnp.float32) for shape in out_shapes],
        in_specs=[pl.BlockSpec(memory_space=pltpu.VMEM)] * len(inputs),
        out_specs=[pl.BlockSpec(memory_space=pltpu.VMEM)] * len(inputs),
        scratch_shapes=scratch,
        compiler_params=pltpu.CompilerParams(
            collective_id=collective_id, has_side_effects=True, vmem_limit_bytes=62 * 1024 * 1024
        ),
        cost_estimate=pl.CostEstimate(flops=moved, transcendentals=0, bytes_accessed=moved * 4),
    )(*inputs)


def pick_rows(table, ids):
    hot = (ids[:, None] == jnp.arange(table.shape[0], dtype=ids.dtype)[None, :]).astype(table.dtype)
    return jnp.dot(hot, table, preferred_element_type=jnp.float32).astype(table.dtype)


def local(entities, relations, head_local, rel_ids, tail_part, tail_local, neg_local):
    factor = 1.0 / math.sqrt(D)
    ent_dev = entities.shape[0]
    columns = entities.shape[1]
    edge_count = head_local.shape[0]
    part_count = lax.axis_size("dom")
    capacity = 2 * edge_count // part_count
    slot_count = part_count * capacity
    relation_count = relations.shape[0]
    head_rows = pick_rows(entities, head_local)
    selectors = [(rel_ids == relation)[:, None] for relation in range(relation_count)]
    query_sum = jnp.zeros((edge_count, columns), jnp.float32)
    for relation in range(relation_count):
        picked = jnp.where(selectors[relation], head_rows, jnp.zeros_like(head_rows))
        query_sum = query_sum + jnp.dot(
            picked, relations[relation], preferred_element_type=jnp.float32
        )
    queries = query_sum.astype(jnp.bfloat16)
    target = tail_part[:, 0]
    target_hot = (target[:, None] == jnp.arange(part_count, dtype=jnp.int32)[None, :]).astype(
        jnp.int32
    )
    earlier = jnp.cumsum(target_hot, axis=0) - target_hot
    position = jnp.sum(earlier * target_hot, axis=1)
    slot_index = target * capacity + position
    slot_match = (slot_index[None, :] == jnp.arange(slot_count, dtype=jnp.int32)[:, None]).astype(
        jnp.int32
    )
    filled = jnp.sum(slot_match, axis=1) > 0
    source = jnp.sum(slot_match * jnp.arange(edge_count, dtype=jnp.int32)[None, :], axis=1)
    send_ids = jnp.where(filled, jnp.take(tail_local, source, axis=0), 0).reshape(
        part_count, capacity
    )
    recv_ids = lax.all_to_all(send_ids, "dom", split_axis=0, concat_axis=0, tiled=True)
    looked_up = pick_rows(entities, recv_ids.reshape(-1)).reshape(
        part_count, capacity, columns
    )
    returned = lax.all_to_all(looked_up, "dom", split_axis=0, concat_axis=0, tiled=True)
    tail_embed = pick_rows(returned.reshape(slot_count, columns), slot_index)
    own_negs = jnp.take(entities, neg_local, axis=0)
    negatives = lax.all_gather(own_negs, "dom", axis=0, tiled=True)
    positive = (
        jnp.sum(queries.astype(jnp.float32) * tail_embed.astype(jnp.float32), axis=1) * factor
    )
    scores = (
        lax.dot_general(
            queries, negatives, (((1,), (1,)), ((), ())), preferred_element_type=jnp.float32
        )
        * factor
    )
    row_max = jnp.maximum(positive, jnp.max(scores, axis=1))
    exp_pos = jnp.exp(positive - row_max)
    exp_neg = jnp.exp(scores - row_max[:, None])
    partition_sum = exp_pos + jnp.sum(exp_neg, axis=1)
    edge_loss = jnp.log(partition_sum) + row_max - positive
    prob_pos = exp_pos / partition_sum
    prob_neg = (exp_neg / partition_sum[:, None]).astype(jnp.bfloat16)
    mixed = jnp.dot(prob_neg, negatives, preferred_element_type=jnp.float32)
    query_grad = (
        factor * ((prob_pos - 1.0)[:, None] * tail_embed.astype(jnp.float32) + mixed)
    ).astype(jnp.bfloat16)
    tail_grad = factor * (prob_pos - 1.0)[:, None] * queries.astype(jnp.float32)
    head_grad = jnp.zeros((edge_count, columns), jnp.float32)
    rel_terms = []
    for relation in range(relation_count):
        picked_grad = jnp.where(selectors[relation], query_grad, jnp.zeros_like(query_grad))
        head_grad = head_grad + lax.dot_general(
            picked_grad,
            relations[relation],
            (((1,), (1,)), ((), ())),
            preferred_element_type=jnp.float32,
        )
        picked_rows = jnp.where(selectors[relation], head_rows, jnp.zeros_like(head_rows))
        rel_terms.append(
            lax.dot_general(
                picked_rows,
                query_grad,
                (((0,), (0,)), ((), ())),
                preferred_element_type=jnp.float32,
            )
        )
    rel_stack, prob_neg_late, queries_late = lax.optimization_barrier(
        (jnp.stack(rel_terms), prob_neg, queries)
    )
    neg_grad = factor * lax.dot_general(
        prob_neg_late, queries_late, (((0,), (0,)), ((), ())), preferred_element_type=jnp.float32
    )
    scale = factor * (prob_pos - 1.0)
    scale_hi = lax.reduce_precision(scale, exponent_bits=8, mantissa_bits=7)
    scale_rest = scale - scale_hi
    scale_mid = lax.reduce_precision(scale_rest, exponent_bits=8, mantissa_bits=7)
    scale_lo = scale_rest - scale_mid
    pack = jnp.concatenate(
        [
            queries,
            jnp.stack([scale_hi, scale_mid, scale_lo], axis=1).astype(jnp.bfloat16),
            jnp.zeros((edge_count, 125), jnp.bfloat16),
        ],
        axis=1,
    )
    pack_send = jnp.dot(
        slot_match.astype(jnp.bfloat16), pack, preferred_element_type=jnp.float32
    ).astype(jnp.bfloat16)
    pack_recv = lax.all_to_all(
        pack_send.reshape(part_count, capacity, pack.shape[1]),
        "dom",
        split_axis=0,
        concat_axis=0,
        tiled=True,
    ).reshape(slot_count, pack.shape[1])
    recv_scale = (
        pack_recv[:, columns].astype(jnp.float32) + pack_recv[:, columns + 1].astype(jnp.float32)
    ) + pack_recv[:, columns + 2].astype(jnp.float32)
    grad_recv = recv_scale[:, None] * pack_recv[:, :columns].astype(jnp.float32)
    rep_count = lax.axis_size("rep")
    neg_order = neg_grad.reshape(part_count // 8, 4, 2, rep_count, -1, columns)
    neg_order = neg_order.transpose(2, 3, 1, 0, 4, 5).reshape(-1, columns)
    orders = (("core", "x", "y", "z"), ("core", "y", "x", "z"))
    width = columns // len(orders)
    lanes = [(0, width * i, width, order, order[::-1]) for i, order in enumerate(orders)]
    lanes.append((1, 0, columns, ("core", "y", "x", "z"), ()))
    relation_flat, owned = lane_reduce([rel_stack.reshape(-1, columns), neg_order], lanes, 0)
    relation_grad = relation_flat.reshape(rel_stack.shape)
    neg_rows = owned.shape[0]
    neg_ids = lax.dynamic_slice_in_dim(neg_local, lax.axis_index("rep") * neg_rows, neg_rows)
    target_ids = jnp.concatenate([head_local, recv_ids.reshape(-1), neg_ids])
    target_rows = jnp.concatenate(
        [head_grad, grad_recv.reshape(slot_count, columns), owned], axis=0
    )
    block_rows = min(512, ent_dev)
    block_count = ent_dev // block_rows

    def add_block(start):
        hot = (
            target_ids[None, :] == (start + jnp.arange(block_rows, dtype=jnp.int32))[:, None]
        ).astype(jnp.float32)
        return jnp.dot(
            hot, target_rows, precision=lax.Precision.HIGHEST, preferred_element_type=jnp.float32
        )

    local_grad = lax.map(add_block, jnp.arange(block_count, dtype=jnp.int32) * block_rows).reshape(
        ent_dev, columns
    )
    entity_grad = tree_reduce(local_grad, ("y",), ("y",), 2)
    return (entity_grad, relation_grad, edge_loss)


def solution(mesh):
    return jax.shard_map(
        local,
        mesh=mesh,
        in_specs=(
            P("dom", None),
            P(),
            P(("dom", "rep")),
            P(("dom", "rep")),
            P(("dom", "rep"), None),
            P(("dom", "rep")),
            P("dom"),
        ),
        out_specs=(P("dom", None), P(), P(("dom", "rep"))),
        check_vma=False,
    )
```

```python
import functools
import math

import jax
import jax.numpy as jnp
from jax import lax
from jax.experimental import pallas as pl
from jax.experimental.pallas import tpu as pltpu
from jax.sharding import PartitionSpec as P

D = 512


def _stage(name, dom, rep, n_dom, n_rep):
    core, xx, zz = dom % 2, (dom // 2) % 4, dom // 8
    if name == "core":
        return 2, core, lambda j: ((zz * 4 + xx) * 2 + j, rep)
    if name == "x":
        return min(4, n_dom // 2), xx, lambda j: ((zz * 4 + j) * 2 + core, rep)
    if name == "y":
        return n_rep, rep, lambda j: (dom, j)
    return max(1, n_dom // 8), zz, lambda j: ((j * 4 + xx) * 2 + core, rep)


def _sum_rows(parts, dst, rows):
    step = min(rows, 64)

    def body(i, carry):
        at = pl.ds(pl.multiple_of(i * step, 8), step)
        total = parts[0](at)
        for part in parts[1:]:
            total = total + part(at)
        dst[at, :] = total
        return carry

    lax.fori_loop(0, rows // step, body, 0)


def _reduce_kernel(rs, ag, sizes, x_ref, out_ref, *scratch):
    n_dom, n_rep = sizes
    dom = lax.axis_index("dom")
    rep = lax.axis_index("rep")
    mesh_id = pl.DeviceIdType.MESH
    rs_info = [_stage(n, dom, rep, n_dom, n_rep) for n in rs]
    ag_info = [_stage(n, dom, rep, n_dom, n_rep) for n in ag]
    nr = len(rs)
    recv_bufs = scratch[:nr]
    acc_bufs = scratch[nr : 2 * nr]
    full = scratch[2 * nr]
    rs_send, rs_recv, ag_send, ag_recv = scratch[2 * nr + 1 : 2 * nr + 5]

    barrier = pltpu.get_barrier_semaphore()
    greeted = 0
    seen = set()
    for name, (g, c, peer) in zip(list(rs) + list(ag), rs_info + ag_info):
        if name in seen:
            continue
        seen.add(name)
        for k in range(1, g):
            pl.semaphore_signal(barrier, 1, device_id=peer((c + k) % g), device_id_type=mesh_id)
            greeted += 1
    pl.semaphore_wait(barrier, greeted)

    sends = []
    src = x_ref
    length = x_ref.shape[0]
    base = 0
    si = 0
    for s, (g, c, peer) in enumerate(rs_info):
        piece = length // g
        for k in range(1, g):
            j = (c + k) % g
            cp = pltpu.make_async_remote_copy(
                src_ref=src.at[pl.ds(pl.multiple_of(j * piece, 8), piece)],
                dst_ref=recv_bufs[s].at[g - k - 1],
                send_sem=rs_send.at[si + k - 1],
                recv_sem=rs_recv.at[si + g - k - 1],
                device_id=peer(j),
                device_id_type=mesh_id,
            )
            cp.start()
            sends.append(cp)
        for k in range(1, g):
            j = (c + k) % g
            pltpu.make_async_remote_copy(
                src_ref=src.at[pl.ds(0, piece)],
                dst_ref=recv_bufs[s].at[k - 1],
                send_sem=rs_send.at[si + k - 1],
                recv_sem=rs_recv.at[si + k - 1],
                device_id=peer(j),
                device_id_type=mesh_id,
            ).wait_recv()
        own = pl.multiple_of(c * piece, 8)
        parts = [lambda at, src=src, own=own: src[pl.ds(own + at.start, at.size), :]]
        for k in range(1, g):
            parts.append(lambda at, b=recv_bufs[s], k=k: b[k - 1, at, :])
        _sum_rows(parts, acc_bufs[s], piece)
        src = acc_bufs[s]
        base = base + c * piece
        length = piece
        si += g - 1

    if not ag_info:
        out_ref[...] = src[...]
    else:
        full[pl.ds(pl.multiple_of(base, 8), length), :] = src[...]
        ai = 0
        for g, c, peer in ag_info:
            mine = pl.ds(pl.multiple_of(base, 8), length)
            for k in range(1, g):
                j = (c + k) % g
                cp = pltpu.make_async_remote_copy(
                    src_ref=full.at[mine],
                    dst_ref=full.at[mine],
                    send_sem=ag_send.at[ai + k - 1],
                    recv_sem=ag_recv.at[ai + g - k - 1],
                    device_id=peer(j),
                    device_id_type=mesh_id,
                )
                cp.start()
                sends.append(cp)
            start = base - c * length
            for k in range(1, g):
                j = (c + k) % g
                theirs = pl.ds(pl.multiple_of(start + j * length, 8), length)
                pltpu.make_async_remote_copy(
                    src_ref=full.at[theirs],
                    dst_ref=full.at[theirs],
                    send_sem=ag_send.at[ai + k - 1],
                    recv_sem=ag_recv.at[ai + k - 1],
                    device_id=peer(j),
                    device_id_type=mesh_id,
                ).wait_recv()
            base = start
            length = length * g
            ai += g - 1
        out_ref[...] = full[...]
    for cp in sends:
        cp.wait_send()


def tree_reduce(x, rs, ag, collective_id):
    n_dom = lax.axis_size("dom")
    n_rep = lax.axis_size("rep")
    rows, columns = x.shape
    shapes = []
    length = rows
    rs_sizes = []
    for name in rs:
        g = _stage(name, 0, 0, n_dom, n_rep)[0]
        rs_sizes.append(g)
    accs = []
    for g in rs_sizes:
        piece = length // g
        shapes.append(pltpu.VMEM((max(g - 1, 1), piece, columns), jnp.float32))
        accs.append(pltpu.VMEM((piece, columns), jnp.float32))
        length = piece
    n_ag = sum(_stage(name, 0, 0, n_dom, n_rep)[0] - 1 for name in ag)
    out_rows = rows if ag else length
    scratch = shapes + accs + [
        pltpu.VMEM((rows if ag else 8, columns), jnp.float32),
        pltpu.SemaphoreType.DMA((max(1, sum(g - 1 for g in rs_sizes)),)),
        pltpu.SemaphoreType.DMA((max(1, sum(g - 1 for g in rs_sizes)),)),
        pltpu.SemaphoreType.DMA((max(1, n_ag),)),
        pltpu.SemaphoreType.DMA((max(1, n_ag),)),
    ]
    return pl.pallas_call(
        functools.partial(_reduce_kernel, tuple(rs), tuple(ag), (n_dom, n_rep)),
        out_shape=jax.ShapeDtypeStruct((out_rows, columns), jnp.float32),
        in_specs=[pl.BlockSpec(memory_space=pltpu.VMEM)],
        out_specs=pl.BlockSpec(memory_space=pltpu.VMEM),
        scratch_shapes=scratch,
        compiler_params=pltpu.CompilerParams(
            collective_id=collective_id, has_side_effects=True, vmem_limit_bytes=60 * 1024 * 1024
        ),
        cost_estimate=pl.CostEstimate(
            flops=rows * columns * 2, transcendentals=0, bytes_accessed=rows * columns * 16
        ),
    )(x)


def _lane_kernel(lanes, sizes, n_in, *refs):
    n_dom, n_rep = sizes
    ins = refs[:n_in]
    outs = refs[n_in : 2 * n_in]
    scratch = refs[2 * n_in :]
    dom = lax.axis_index("dom")
    rep = lax.axis_index("rep")
    mesh_id = pl.DeviceIdType.MESH
    pos = 0
    lane_bufs = []
    for _, _, _, rs, _ in lanes:
        lane_bufs.append((scratch[pos : pos + len(rs)], scratch[pos + len(rs) : pos + 2 * len(rs)]))
        pos += 2 * len(rs)
    fulls = scratch[pos : pos + n_in]
    rs_send, rs_recv, ag_send, ag_recv = scratch[pos + n_in : pos + n_in + 4]

    def info(name):
        return _stage(name, dom, rep, n_dom, n_rep)

    barrier = pltpu.get_barrier_semaphore()
    greeted = 0
    names = []
    for lane in lanes:
        for name in lane[3] + lane[4]:
            if name not in names:
                names.append(name)
    for name in names:
        g, c, peer = info(name)
        for k in range(1, g):
            pl.semaphore_signal(barrier, 1, device_id=peer((c + k) % g), device_id_type=mesh_id)
            greeted += 1
    pl.semaphore_wait(barrier, greeted)

    sends = []
    state = [
        (ins[i], c0, w, ins[i].shape[0], 0) for i, c0, w, _, _ in lanes
    ]
    rs_base = []
    total = 0
    for lane in lanes:
        rs_base.append(total)
        total += sum(info(name)[0] - 1 for name in lane[3])
    for t in range(max(len(lane[3]) for lane in lanes)):
        pending = []
        offsets = [rs_base[li] + sum(info(n)[0] - 1 for n in lane[3][:t]) for li, lane in enumerate(lanes)]
        for li, lane in enumerate(lanes):
            if t >= len(lane[3]):
                continue
            g, c, peer = info(lane[3][t])
            ref, c0, w, length, gbase = state[li]
            piece = length // g
            si = offsets[li]
            recv = lane_bufs[li][0][t]
            for k in range(1, g):
                j = (c + k) % g
                cp = pltpu.make_async_remote_copy(
                    src_ref=ref.at[pl.ds(pl.multiple_of(j * piece, 8), piece), pl.ds(c0, w)],
                    dst_ref=recv.at[g - k - 1],
                    send_sem=rs_send.at[si + k - 1],
                    recv_sem=rs_recv.at[si + g - k - 1],
                    device_id=peer(j),
                    device_id_type=mesh_id,
                )
                cp.start()
                sends.append(cp)
            pending.append(li)
        for li in pending:
            lane = lanes[li]
            g, c, peer = info(lane[3][t])
            ref, c0, w, length, gbase = state[li]
            piece = length // g
            si = offsets[li]
            recv = lane_bufs[li][0][t]
            acc = lane_bufs[li][1][t]
            for k in range(1, g):
                j = (c + k) % g
                pltpu.make_async_remote_copy(
                    src_ref=ref.at[pl.ds(0, piece), pl.ds(c0, w)],
                    dst_ref=recv.at[k - 1],
                    send_sem=rs_send.at[si + k - 1],
                    recv_sem=rs_recv.at[si + k - 1],
                    device_id=peer(j),
                    device_id_type=mesh_id,
                ).wait_recv()
            own = pl.multiple_of(c * piece, 8)
            parts = [lambda at, ref=ref, own=own, c0=c0, w=w: ref[pl.ds(own + at.start, at.size), pl.ds(c0, w)]]
            for k in range(1, g):
                parts.append(lambda at, b=recv, k=k: b[k - 1, at, :])
            _sum_rows(parts, acc, piece)
            state[li] = (acc, 0, w, piece, gbase + c * piece)

    ag_state = []
    for li, lane in enumerate(lanes):
        acc, _, w, length, gbase = state[li]
        i, c0 = lane[0], lane[1]
        if lane[4]:
            fulls[i][pl.ds(pl.multiple_of(gbase, 8), length), pl.ds(c0, w)] = acc[...]
        else:
            outs[i][...] = acc[...]
        ag_state.append((length, gbase))
    ag_base = []
    total = 0
    for lane in lanes:
        ag_base.append(total)
        total += sum(info(name)[0] - 1 for name in lane[4])
    for t in range(max(len(lane[4]) for lane in lanes)):
        pending = []
        offsets = [ag_base[li] + sum(info(n)[0] - 1 for n in lane[4][:t]) for li, lane in enumerate(lanes)]
        for li, lane in enumerate(lanes):
            if t >= len(lane[4]):
                continue
            g, c, peer = info(lane[4][t])
            length, gbase = ag_state[li]
            full = fulls[lane[0]]
            cols = pl.ds(lane[1], lane[2])
            mine = pl.ds(pl.multiple_of(gbase, 8), length)
            ai = offsets[li]
            for k in range(1, g):
                j = (c + k) % g
                cp = pltpu.make_async_remote_copy(
                    src_ref=full.at[mine, cols],
                    dst_ref=full.at[mine, cols],
                    send_sem=ag_send.at[ai + k - 1],
                    recv_sem=ag_recv.at[ai + g - k - 1],
                    device_id=peer(j),
                    device_id_type=mesh_id,
                )
                cp.start()
                sends.append(cp)
            pending.append(li)
        for li in pending:
            lane = lanes[li]
            g, c, peer = info(lane[4][t])
            length, gbase = ag_state[li]
            full = fulls[lane[0]]
            cols = pl.ds(lane[1], lane[2])
            ai = offsets[li]
            start = gbase - c * length
            for k in range(1, g):
                j = (c + k) % g
                theirs = pl.ds(pl.multiple_of(start + j * length, 8), length)
                pltpu.make_async_remote_copy(
                    src_ref=full.at[theirs, cols],
                    dst_ref=full.at[theirs, cols],
                    send_sem=ag_send.at[ai + k - 1],
                    recv_sem=ag_recv.at[ai + k - 1],
                    device_id=peer(j),
                    device_id_type=mesh_id,
                ).wait_recv()
            ag_state[li] = (length * g, start)
    gathered = sorted({lane[0] for lane in lanes if lane[4]})
    for i in gathered:
        outs[i][...] = fulls[i][...]
    for cp in sends:
        cp.wait_send()


def lane_reduce(inputs, lanes, collective_id):
    n_dom = lax.axis_size("dom")
    n_rep = lax.axis_size("rep")
    scratch = []
    recv_shapes, acc_shapes = [], []
    n_rs = n_ag = 0
    out_shapes = [None] * len(inputs)
    for i, c0, w, rs, ag in lanes:
        length = inputs[i].shape[0]
        recv, accs = [], []
        for name in rs:
            g = _stage(name, 0, 0, n_dom, n_rep)[0]
            piece = length // g
            recv.append(pltpu.VMEM((max(g - 1, 1), piece, w), jnp.float32))
            accs.append(pltpu.VMEM((piece, w), jnp.float32))
            length = piece
            n_rs += g - 1
        n_ag += sum(_stage(name, 0, 0, n_dom, n_rep)[0] - 1 for name in ag)
        scratch += recv + accs
        out_shapes[i] = inputs[i].shape if ag else (length, w)
    for i, x in enumerate(inputs):
        scratch.append(pltpu.VMEM(x.shape if any(l[0] == i and l[4] for l in lanes) else (8, 128), jnp.float32))
    scratch += [
        pltpu.SemaphoreType.DMA((max(1, n_rs),)),
        pltpu.SemaphoreType.DMA((max(1, n_rs),)),
        pltpu.SemaphoreType.DMA((max(1, n_ag),)),
        pltpu.SemaphoreType.DMA((max(1, n_ag),)),
    ]
    moved = sum(x.size for x in inputs) * 4
    return pl.pallas_call(
        functools.partial(_lane_kernel, tuple(lanes), (n_dom, n_rep), len(inputs)),
        out_shape=[jax.ShapeDtypeStruct(shape, jnp.float32) for shape in out_shapes],
        in_specs=[pl.BlockSpec(memory_space=pltpu.VMEM)] * len(inputs),
        out_specs=[pl.BlockSpec(memory_space=pltpu.VMEM)] * len(inputs),
        scratch_shapes=scratch,
        compiler_params=pltpu.CompilerParams(
            collective_id=collective_id, has_side_effects=True, vmem_limit_bytes=62 * 1024 * 1024
        ),
        cost_estimate=pl.CostEstimate(flops=moved, transcendentals=0, bytes_accessed=moved * 4),
    )(*inputs)


def pick_rows(table, ids):
    hot = (ids[:, None] == jnp.arange(table.shape[0], dtype=ids.dtype)[None, :]).astype(table.dtype)
    return jnp.dot(hot, table, preferred_element_type=jnp.float32).astype(table.dtype)


def local(entities, relations, head_local, rel_ids, tail_part, tail_local, neg_local):
    factor = 1.0 / math.sqrt(D)
    ent_dev = entities.shape[0]
    columns = entities.shape[1]
    edge_count = head_local.shape[0]
    part_count = lax.axis_size("dom")
    capacity = 2 * edge_count // part_count
    slot_count = part_count * capacity
    relation_count = relations.shape[0]
    head_rows = pick_rows(entities, head_local)
    selectors = [(rel_ids == relation)[:, None] for relation in range(relation_count)]
    query_sum = jnp.zeros((edge_count, columns), jnp.float32)
    for relation in range(relation_count):
        picked = jnp.where(selectors[relation], head_rows, jnp.zeros_like(head_rows))
        query_sum = query_sum + jnp.dot(
            picked, relations[relation], preferred_element_type=jnp.float32
        )
    queries = query_sum.astype(jnp.bfloat16)
    target = tail_part[:, 0]
    target_hot = (target[:, None] == jnp.arange(part_count, dtype=jnp.int32)[None, :]).astype(
        jnp.int32
    )
    earlier = jnp.cumsum(target_hot, axis=0) - target_hot
    position = jnp.sum(earlier * target_hot, axis=1)
    slot_index = target * capacity + position
    slot_match = (slot_index[None, :] == jnp.arange(slot_count, dtype=jnp.int32)[:, None]).astype(
        jnp.int32
    )
    filled = jnp.sum(slot_match, axis=1) > 0
    source = jnp.sum(slot_match * jnp.arange(edge_count, dtype=jnp.int32)[None, :], axis=1)
    send_ids = jnp.sum(slot_match * tail_local[None, :], axis=1).reshape(part_count, capacity)
    recv_ids = lax.all_to_all(send_ids, "dom", split_axis=0, concat_axis=0, tiled=True)
    looked_up = pick_rows(entities, recv_ids.reshape(-1)).reshape(
        part_count, capacity, columns
    )
    returned = lax.all_to_all(looked_up, "dom", split_axis=0, concat_axis=0, tiled=True)
    tail_embed = pick_rows(returned.reshape(slot_count, columns), slot_index)
    own_negs = pick_rows(entities, neg_local)
    negatives = lax.all_gather(own_negs, "dom", axis=0, tiled=True)
    positive = (
        jnp.sum(queries.astype(jnp.float32) * tail_embed.astype(jnp.float32), axis=1) * factor
    )
    scores = (
        lax.dot_general(
            queries, negatives, (((1,), (1,)), ((), ())), preferred_element_type=jnp.float32
        )
        * factor
    )
    row_max = jnp.maximum(positive, jnp.max(scores, axis=1))
    exp_pos = jnp.exp(positive - row_max)
    exp_neg = jnp.exp(scores - row_max[:, None])
    partition_sum = exp_pos + jnp.sum(exp_neg, axis=1)
    edge_loss = jnp.log(partition_sum) + row_max - positive
    prob_pos = exp_pos / partition_sum
    prob_neg = (exp_neg / partition_sum[:, None]).astype(jnp.bfloat16)
    mixed = jnp.dot(prob_neg, negatives, preferred_element_type=jnp.float32)
    query_grad = (
        factor * ((prob_pos - 1.0)[:, None] * tail_embed.astype(jnp.float32) + mixed)
    ).astype(jnp.bfloat16)
    tail_grad = factor * (prob_pos - 1.0)[:, None] * queries.astype(jnp.float32)
    head_grad = jnp.zeros((edge_count, columns), jnp.float32)
    rel_terms = []
    for relation in range(relation_count):
        picked_grad = jnp.where(selectors[relation], query_grad, jnp.zeros_like(query_grad))
        head_grad = head_grad + lax.dot_general(
            picked_grad,
            relations[relation],
            (((1,), (1,)), ((), ())),
            preferred_element_type=jnp.float32,
        )
        picked_rows = jnp.where(selectors[relation], head_rows, jnp.zeros_like(head_rows))
        rel_terms.append(
            lax.dot_general(
                picked_rows,
                query_grad,
                (((0,), (0,)), ((), ())),
                preferred_element_type=jnp.float32,
            )
        )
    rel_stack, prob_neg_late, queries_late = lax.optimization_barrier(
        (jnp.stack(rel_terms), prob_neg, queries)
    )
    neg_grad = factor * lax.dot_general(
        prob_neg_late, queries_late, (((0,), (0,)), ((), ())), preferred_element_type=jnp.float32
    )
    scale = factor * (prob_pos - 1.0)
    scale_hi = lax.reduce_precision(scale, exponent_bits=8, mantissa_bits=7)
    scale_rest = scale - scale_hi
    scale_mid = lax.reduce_precision(scale_rest, exponent_bits=8, mantissa_bits=7)
    scale_lo = scale_rest - scale_mid
    pack = jnp.concatenate(
        [
            queries,
            jnp.stack([scale_hi, scale_mid, scale_lo], axis=1).astype(jnp.bfloat16),
            jnp.zeros((edge_count, 125), jnp.bfloat16),
        ],
        axis=1,
    )
    pack_send = jnp.dot(
        slot_match.astype(jnp.bfloat16), pack, preferred_element_type=jnp.float32
    ).astype(jnp.bfloat16)
    pack_recv = lax.all_to_all(
        pack_send.reshape(part_count, capacity, pack.shape[1]),
        "dom",
        split_axis=0,
        concat_axis=0,
        tiled=True,
    ).reshape(slot_count, pack.shape[1])
    recv_scale = (
        pack_recv[:, columns].astype(jnp.float32) + pack_recv[:, columns + 1].astype(jnp.float32)
    ) + pack_recv[:, columns + 2].astype(jnp.float32)
    grad_recv = recv_scale[:, None] * pack_recv[:, :columns].astype(jnp.float32)
    rep_count = lax.axis_size("rep")
    neg_order = neg_grad.reshape(part_count // 8, 4, 2, rep_count, -1, columns)
    neg_order = neg_order.transpose(2, 3, 1, 0, 4, 5).reshape(-1, columns)
    orders = (("core", "x", "y", "z"), ("core", "y", "x", "z"))
    width = columns // len(orders)
    lanes = [(0, width * i, width, order, order[::-1]) for i, order in enumerate(orders)]
    lanes.append((1, 0, columns, ("core", "y", "x", "z"), ()))
    relation_flat, owned = lane_reduce([rel_stack.reshape(-1, columns), neg_order], lanes, 0)
    relation_grad = relation_flat.reshape(rel_stack.shape)
    neg_rows = owned.shape[0]
    neg_ids = lax.dynamic_slice_in_dim(neg_local, lax.axis_index("rep") * neg_rows, neg_rows)
    target_ids = jnp.concatenate([head_local, recv_ids.reshape(-1), neg_ids])
    target_rows = jnp.concatenate(
        [head_grad, grad_recv.reshape(slot_count, columns), owned], axis=0
    )
    block_rows = min(512, ent_dev)
    block_count = ent_dev // block_rows

    def add_block(start):
        hot = (
            target_ids[None, :] == (start + jnp.arange(block_rows, dtype=jnp.int32))[:, None]
        ).astype(jnp.float32)
        return jnp.dot(
            hot, target_rows, precision=lax.Precision.HIGHEST, preferred_element_type=jnp.float32
        )

    local_grad = lax.map(add_block, jnp.arange(block_count, dtype=jnp.int32) * block_rows).reshape(
        ent_dev, columns
    )
    entity_grad = tree_reduce(local_grad, ("y",), ("y",), 2)
    return (entity_grad, relation_grad, edge_loss)


def solution(mesh):
    return jax.shard_map(
        local,
        mesh=mesh,
        in_specs=(
            P("dom", None),
            P(),
            P(("dom", "rep")),
            P(("dom", "rep")),
            P(("dom", "rep"), None),
            P(("dom", "rep")),
            P("dom"),
        ),
        out_specs=(P("dom", None), P(), P(("dom", "rep"))),
        check_vma=False,
    )
```

```python
import functools
import math

import jax
import jax.numpy as jnp
from jax import lax
from jax.experimental import pallas as pl
from jax.experimental.pallas import tpu as pltpu
from jax.sharding import PartitionSpec as P

D = 512


def _stage(name, dom, rep, n_dom, n_rep):
    core, xx, zz = dom % 2, (dom // 2) % 4, dom // 8
    if name == "core":
        return 2, core, lambda j: ((zz * 4 + xx) * 2 + j, rep)
    if name == "x":
        return min(4, n_dom // 2), xx, lambda j: ((zz * 4 + j) * 2 + core, rep)
    if name == "y":
        return n_rep, rep, lambda j: (dom, j)
    return max(1, n_dom // 8), zz, lambda j: ((j * 4 + xx) * 2 + core, rep)


def _sum_rows(parts, dst, rows):
    step = min(rows, 64)

    def body(i, carry):
        at = pl.ds(pl.multiple_of(i * step, 8), step)
        total = parts[0](at)
        for part in parts[1:]:
            total = total + part(at)
        dst[at, :] = total
        return carry

    lax.fori_loop(0, rows // step, body, 0)


def _reduce_kernel(rs, ag, sizes, x_ref, out_ref, *scratch):
    n_dom, n_rep = sizes
    dom = lax.axis_index("dom")
    rep = lax.axis_index("rep")
    mesh_id = pl.DeviceIdType.MESH
    rs_info = [_stage(n, dom, rep, n_dom, n_rep) for n in rs]
    ag_info = [_stage(n, dom, rep, n_dom, n_rep) for n in ag]
    nr = len(rs)
    recv_bufs = scratch[:nr]
    acc_bufs = scratch[nr : 2 * nr]
    full = scratch[2 * nr]
    rs_send, rs_recv, ag_send, ag_recv = scratch[2 * nr + 1 : 2 * nr + 5]

    barrier = pltpu.get_barrier_semaphore()
    greeted = 0
    seen = set()
    for name, (g, c, peer) in zip(list(rs) + list(ag), rs_info + ag_info):
        if name in seen:
            continue
        seen.add(name)
        for k in range(1, g):
            pl.semaphore_signal(barrier, 1, device_id=peer((c + k) % g), device_id_type=mesh_id)
            greeted += 1
    pl.semaphore_wait(barrier, greeted)

    sends = []
    src = x_ref
    length = x_ref.shape[0]
    base = 0
    si = 0
    for s, (g, c, peer) in enumerate(rs_info):
        piece = length // g
        for k in range(1, g):
            j = (c + k) % g
            cp = pltpu.make_async_remote_copy(
                src_ref=src.at[pl.ds(pl.multiple_of(j * piece, 8), piece)],
                dst_ref=recv_bufs[s].at[g - k - 1],
                send_sem=rs_send.at[si + k - 1],
                recv_sem=rs_recv.at[si + g - k - 1],
                device_id=peer(j),
                device_id_type=mesh_id,
            )
            cp.start()
            sends.append(cp)
        for k in range(1, g):
            j = (c + k) % g
            pltpu.make_async_remote_copy(
                src_ref=src.at[pl.ds(0, piece)],
                dst_ref=recv_bufs[s].at[k - 1],
                send_sem=rs_send.at[si + k - 1],
                recv_sem=rs_recv.at[si + k - 1],
                device_id=peer(j),
                device_id_type=mesh_id,
            ).wait_recv()
        own = pl.multiple_of(c * piece, 8)
        parts = [lambda at, src=src, own=own: src[pl.ds(own + at.start, at.size), :]]
        for k in range(1, g):
            parts.append(lambda at, b=recv_bufs[s], k=k: b[k - 1, at, :])
        _sum_rows(parts, acc_bufs[s], piece)
        src = acc_bufs[s]
        base = base + c * piece
        length = piece
        si += g - 1

    if not ag_info:
        out_ref[...] = src[...]
    else:
        full[pl.ds(pl.multiple_of(base, 8), length), :] = src[...]
        ai = 0
        for g, c, peer in ag_info:
            mine = pl.ds(pl.multiple_of(base, 8), length)
            for k in range(1, g):
                j = (c + k) % g
                cp = pltpu.make_async_remote_copy(
                    src_ref=full.at[mine],
                    dst_ref=full.at[mine],
                    send_sem=ag_send.at[ai + k - 1],
                    recv_sem=ag_recv.at[ai + g - k - 1],
                    device_id=peer(j),
                    device_id_type=mesh_id,
                )
                cp.start()
                sends.append(cp)
            start = base - c * length
            for k in range(1, g):
                j = (c + k) % g
                theirs = pl.ds(pl.multiple_of(start + j * length, 8), length)
                pltpu.make_async_remote_copy(
                    src_ref=full.at[theirs],
                    dst_ref=full.at[theirs],
                    send_sem=ag_send.at[ai + k - 1],
                    recv_sem=ag_recv.at[ai + k - 1],
                    device_id=peer(j),
                    device_id_type=mesh_id,
                ).wait_recv()
            base = start
            length = length * g
            ai += g - 1
        out_ref[...] = full[...]
    for cp in sends:
        cp.wait_send()


def tree_reduce(x, rs, ag, collective_id):
    n_dom = lax.axis_size("dom")
    n_rep = lax.axis_size("rep")
    rows, columns = x.shape
    shapes = []
    length = rows
    rs_sizes = []
    for name in rs:
        g = _stage(name, 0, 0, n_dom, n_rep)[0]
        rs_sizes.append(g)
    accs = []
    for g in rs_sizes:
        piece = length // g
        shapes.append(pltpu.VMEM((max(g - 1, 1), piece, columns), jnp.float32))
        accs.append(pltpu.VMEM((piece, columns), jnp.float32))
        length = piece
    n_ag = sum(_stage(name, 0, 0, n_dom, n_rep)[0] - 1 for name in ag)
    out_rows = rows if ag else length
    scratch = shapes + accs + [
        pltpu.VMEM((rows if ag else 8, columns), jnp.float32),
        pltpu.SemaphoreType.DMA((max(1, sum(g - 1 for g in rs_sizes)),)),
        pltpu.SemaphoreType.DMA((max(1, sum(g - 1 for g in rs_sizes)),)),
        pltpu.SemaphoreType.DMA((max(1, n_ag),)),
        pltpu.SemaphoreType.DMA((max(1, n_ag),)),
    ]
    return pl.pallas_call(
        functools.partial(_reduce_kernel, tuple(rs), tuple(ag), (n_dom, n_rep)),
        out_shape=jax.ShapeDtypeStruct((out_rows, columns), jnp.float32),
        in_specs=[pl.BlockSpec(memory_space=pltpu.VMEM)],
        out_specs=pl.BlockSpec(memory_space=pltpu.VMEM),
        scratch_shapes=scratch,
        compiler_params=pltpu.CompilerParams(
            collective_id=collective_id, has_side_effects=True, vmem_limit_bytes=60 * 1024 * 1024
        ),
        cost_estimate=pl.CostEstimate(
            flops=rows * columns * 2, transcendentals=0, bytes_accessed=rows * columns * 16
        ),
    )(x)


def _lane_kernel(lanes, sizes, n_in, *refs):
    n_dom, n_rep = sizes
    ins = refs[:n_in]
    outs = refs[n_in : 2 * n_in]
    scratch = refs[2 * n_in :]
    dom = lax.axis_index("dom")
    rep = lax.axis_index("rep")
    mesh_id = pl.DeviceIdType.MESH
    pos = 0
    lane_bufs = []
    for _, _, _, rs, _ in lanes:
        lane_bufs.append((scratch[pos : pos + len(rs)], scratch[pos + len(rs) : pos + 2 * len(rs)]))
        pos += 2 * len(rs)
    fulls = scratch[pos : pos + n_in]
    rs_send, rs_recv, ag_send, ag_recv = scratch[pos + n_in : pos + n_in + 4]

    def info(name):
        return _stage(name, dom, rep, n_dom, n_rep)

    barrier = pltpu.get_barrier_semaphore()
    greeted = 0
    names = []
    for lane in lanes:
        for name in lane[3] + lane[4]:
            if name not in names:
                names.append(name)
    for name in names:
        g, c, peer = info(name)
        for k in range(1, g):
            pl.semaphore_signal(barrier, 1, device_id=peer((c + k) % g), device_id_type=mesh_id)
            greeted += 1
    pl.semaphore_wait(barrier, greeted)

    sends = []
    state = [
        (ins[i], c0, w, ins[i].shape[0], 0) for i, c0, w, _, _ in lanes
    ]
    rs_base = []
    total = 0
    for lane in lanes:
        rs_base.append(total)
        total += sum(info(name)[0] - 1 for name in lane[3])
    for t in range(max(len(lane[3]) for lane in lanes)):
        pending = []
        offsets = [rs_base[li] + sum(info(n)[0] - 1 for n in lane[3][:t]) for li, lane in enumerate(lanes)]
        for li, lane in enumerate(lanes):
            if t >= len(lane[3]):
                continue
            g, c, peer = info(lane[3][t])
            ref, c0, w, length, gbase = state[li]
            piece = length // g
            si = offsets[li]
            recv = lane_bufs[li][0][t]
            for k in range(1, g):
                j = (c + k) % g
                cp = pltpu.make_async_remote_copy(
                    src_ref=ref.at[pl.ds(pl.multiple_of(j * piece, 8), piece), pl.ds(c0, w)],
                    dst_ref=recv.at[g - k - 1],
                    send_sem=rs_send.at[si + k - 1],
                    recv_sem=rs_recv.at[si + g - k - 1],
                    device_id=peer(j),
                    device_id_type=mesh_id,
                )
                cp.start()
                sends.append(cp)
            pending.append(li)
        for li in pending:
            lane = lanes[li]
            g, c, peer = info(lane[3][t])
            ref, c0, w, length, gbase = state[li]
            piece = length // g
            si = offsets[li]
            recv = lane_bufs[li][0][t]
            acc = lane_bufs[li][1][t]
            for k in range(1, g):
                j = (c + k) % g
                pltpu.make_async_remote_copy(
                    src_ref=ref.at[pl.ds(0, piece), pl.ds(c0, w)],
                    dst_ref=recv.at[k - 1],
                    send_sem=rs_send.at[si + k - 1],
                    recv_sem=rs_recv.at[si + k - 1],
                    device_id=peer(j),
                    device_id_type=mesh_id,
                ).wait_recv()
            own = pl.multiple_of(c * piece, 8)
            parts = [lambda at, ref=ref, own=own, c0=c0, w=w: ref[pl.ds(own + at.start, at.size), pl.ds(c0, w)]]
            for k in range(1, g):
                parts.append(lambda at, b=recv, k=k: b[k - 1, at, :])
            _sum_rows(parts, acc, piece)
            state[li] = (acc, 0, w, piece, gbase + c * piece)

    ag_state = []
    for li, lane in enumerate(lanes):
        acc, _, w, length, gbase = state[li]
        i, c0 = lane[0], lane[1]
        if lane[4]:
            fulls[i][pl.ds(pl.multiple_of(gbase, 8), length), pl.ds(c0, w)] = acc[...]
        else:
            outs[i][...] = acc[...]
        ag_state.append((length, gbase))
    ag_base = []
    total = 0
    for lane in lanes:
        ag_base.append(total)
        total += sum(info(name)[0] - 1 for name in lane[4])
    for t in range(max(len(lane[4]) for lane in lanes)):
        pending = []
        offsets = [ag_base[li] + sum(info(n)[0] - 1 for n in lane[4][:t]) for li, lane in enumerate(lanes)]
        for li, lane in enumerate(lanes):
            if t >= len(lane[4]):
                continue
            g, c, peer = info(lane[4][t])
            length, gbase = ag_state[li]
            full = fulls[lane[0]]
            cols = pl.ds(lane[1], lane[2])
            mine = pl.ds(pl.multiple_of(gbase, 8), length)
            ai = offsets[li]
            for k in range(1, g):
                j = (c + k) % g
                cp = pltpu.make_async_remote_copy(
                    src_ref=full.at[mine, cols],
                    dst_ref=full.at[mine, cols],
                    send_sem=ag_send.at[ai + k - 1],
                    recv_sem=ag_recv.at[ai + g - k - 1],
                    device_id=peer(j),
                    device_id_type=mesh_id,
                )
                cp.start()
                sends.append(cp)
            pending.append(li)
        for li in pending:
            lane = lanes[li]
            g, c, peer = info(lane[4][t])
            length, gbase = ag_state[li]
            full = fulls[lane[0]]
            cols = pl.ds(lane[1], lane[2])
            ai = offsets[li]
            start = gbase - c * length
            for k in range(1, g):
                j = (c + k) % g
                theirs = pl.ds(pl.multiple_of(start + j * length, 8), length)
                pltpu.make_async_remote_copy(
                    src_ref=full.at[theirs, cols],
                    dst_ref=full.at[theirs, cols],
                    send_sem=ag_send.at[ai + k - 1],
                    recv_sem=ag_recv.at[ai + k - 1],
                    device_id=peer(j),
                    device_id_type=mesh_id,
                ).wait_recv()
            ag_state[li] = (length * g, start)
    gathered = sorted({lane[0] for lane in lanes if lane[4]})
    for i in gathered:
        outs[i][...] = fulls[i][...]
    for cp in sends:
        cp.wait_send()


def lane_reduce(inputs, lanes, collective_id):
    n_dom = lax.axis_size("dom")
    n_rep = lax.axis_size("rep")
    scratch = []
    recv_shapes, acc_shapes = [], []
    n_rs = n_ag = 0
    out_shapes = [None] * len(inputs)
    for i, c0, w, rs, ag in lanes:
        length = inputs[i].shape[0]
        recv, accs = [], []
        for name in rs:
            g = _stage(name, 0, 0, n_dom, n_rep)[0]
            piece = length // g
            recv.append(pltpu.VMEM((max(g - 1, 1), piece, w), jnp.float32))
            accs.append(pltpu.VMEM((piece, w), jnp.float32))
            length = piece
            n_rs += g - 1
        n_ag += sum(_stage(name, 0, 0, n_dom, n_rep)[0] - 1 for name in ag)
        scratch += recv + accs
        out_shapes[i] = inputs[i].shape if ag else (length, w)
    for i, x in enumerate(inputs):
        scratch.append(pltpu.VMEM(x.shape if any(l[0] == i and l[4] for l in lanes) else (8, 128), jnp.float32))
    scratch += [
        pltpu.SemaphoreType.DMA((max(1, n_rs),)),
        pltpu.SemaphoreType.DMA((max(1, n_rs),)),
        pltpu.SemaphoreType.DMA((max(1, n_ag),)),
        pltpu.SemaphoreType.DMA((max(1, n_ag),)),
    ]
    moved = sum(x.size for x in inputs) * 4
    return pl.pallas_call(
        functools.partial(_lane_kernel, tuple(lanes), (n_dom, n_rep), len(inputs)),
        out_shape=[jax.ShapeDtypeStruct(shape, jnp.float32) for shape in out_shapes],
        in_specs=[pl.BlockSpec(memory_space=pltpu.VMEM)] * len(inputs),
        out_specs=[pl.BlockSpec(memory_space=pltpu.VMEM)] * len(inputs),
        scratch_shapes=scratch,
        compiler_params=pltpu.CompilerParams(
            collective_id=collective_id, has_side_effects=True, vmem_limit_bytes=62 * 1024 * 1024
        ),
        cost_estimate=pl.CostEstimate(flops=moved, transcendentals=0, bytes_accessed=moved * 4),
    )(*inputs)


def pick_rows(table, ids):
    hot = (ids[:, None] == jnp.arange(table.shape[0], dtype=ids.dtype)[None, :]).astype(table.dtype)
    return jnp.dot(hot, table, preferred_element_type=jnp.float32).astype(table.dtype)


def local(entities, relations, head_local, rel_ids, tail_part, tail_local, neg_local):
    factor = 1.0 / math.sqrt(D)
    ent_dev = entities.shape[0]
    columns = entities.shape[1]
    edge_count = head_local.shape[0]
    part_count = lax.axis_size("dom")
    capacity = 2 * edge_count // part_count
    slot_count = part_count * capacity
    relation_count = relations.shape[0]
    head_rows = pick_rows(entities, head_local)
    selectors = [(rel_ids == relation)[:, None] for relation in range(relation_count)]
    query_sum = jnp.zeros((edge_count, columns), jnp.float32)
    for relation in range(relation_count):
        picked = jnp.where(selectors[relation], head_rows, jnp.zeros_like(head_rows))
        query_sum = query_sum + jnp.dot(
            picked, relations[relation], preferred_element_type=jnp.float32
        )
    queries = query_sum.astype(jnp.bfloat16)
    target = tail_part[:, 0]
    target_hot = (target[:, None] == jnp.arange(part_count, dtype=jnp.int32)[None, :]).astype(
        jnp.int32
    )
    earlier = jnp.cumsum(target_hot, axis=0) - target_hot
    position = jnp.sum(earlier * target_hot, axis=1)
    slot_index = target * capacity + position
    slot_match = (slot_index[None, :] == jnp.arange(slot_count, dtype=jnp.int32)[:, None]).astype(
        jnp.int32
    )
    filled = jnp.sum(slot_match, axis=1) > 0
    source = jnp.sum(slot_match * jnp.arange(edge_count, dtype=jnp.int32)[None, :], axis=1)
    send_ids = jnp.sum(slot_match * tail_local[None, :], axis=1).reshape(part_count, capacity)
    recv_ids = lax.all_to_all(send_ids, "dom", split_axis=0, concat_axis=0, tiled=True)
    looked_up = pick_rows(entities, recv_ids.reshape(-1)).reshape(
        part_count, capacity, columns
    )
    returned = lax.all_to_all(looked_up, "dom", split_axis=0, concat_axis=0, tiled=True)
    tail_embed = pick_rows(returned.reshape(slot_count, columns), slot_index)
    own_negs = pick_rows(entities, neg_local)
    negatives = lax.all_gather(own_negs, "dom", axis=0, tiled=True)
    positive = (
        jnp.sum(queries.astype(jnp.float32) * tail_embed.astype(jnp.float32), axis=1) * factor
    )
    scores = (
        lax.dot_general(
            queries, negatives, (((1,), (1,)), ((), ())), preferred_element_type=jnp.float32
        )
        * factor
    )
    row_max = jnp.maximum(positive, jnp.max(scores, axis=1))
    exp_pos = jnp.exp(positive - row_max)
    exp_neg = jnp.exp(scores - row_max[:, None])
    partition_sum = exp_pos + jnp.sum(exp_neg, axis=1)
    edge_loss = jnp.log(partition_sum) + row_max - positive
    prob_pos = exp_pos / partition_sum
    prob_neg = (exp_neg / partition_sum[:, None]).astype(jnp.bfloat16)
    mixed = jnp.dot(prob_neg, negatives, preferred_element_type=jnp.float32)
    query_grad = (
        factor * ((prob_pos - 1.0)[:, None] * tail_embed.astype(jnp.float32) + mixed)
    ).astype(jnp.bfloat16)
    tail_grad = factor * (prob_pos - 1.0)[:, None] * queries.astype(jnp.float32)
    head_grad = jnp.zeros((edge_count, columns), jnp.float32)
    rel_terms = []
    for relation in range(relation_count):
        picked_grad = jnp.where(selectors[relation], query_grad, jnp.zeros_like(query_grad))
        head_grad = head_grad + lax.dot_general(
            picked_grad,
            relations[relation],
            (((1,), (1,)), ((), ())),
            preferred_element_type=jnp.float32,
        )
        picked_rows = jnp.where(selectors[relation], head_rows, jnp.zeros_like(head_rows))
        rel_terms.append(
            lax.dot_general(
                picked_rows,
                query_grad,
                (((0,), (0,)), ((), ())),
                preferred_element_type=jnp.float32,
            )
        )
    rel_stack, prob_neg_late, queries_late = lax.optimization_barrier(
        (jnp.stack(rel_terms), prob_neg, queries)
    )
    neg_grad = factor * lax.dot_general(
        prob_neg_late, queries_late, (((0,), (0,)), ((), ())), preferred_element_type=jnp.float32
    )
    scale = factor * (prob_pos - 1.0)
    scale_hi = lax.reduce_precision(scale, exponent_bits=8, mantissa_bits=7)
    scale_rest = scale - scale_hi
    scale_mid = lax.reduce_precision(scale_rest, exponent_bits=8, mantissa_bits=7)
    scale_lo = scale_rest - scale_mid
    pack = jnp.concatenate(
        [
            queries,
            jnp.stack([scale_hi, scale_mid, scale_lo], axis=1).astype(jnp.bfloat16),
            jnp.zeros((edge_count, 125), jnp.bfloat16),
        ],
        axis=1,
    )
    pack_send = jnp.dot(
        slot_match.astype(jnp.bfloat16), pack, preferred_element_type=jnp.float32
    ).astype(jnp.bfloat16)
    pack_recv = lax.all_to_all(
        pack_send.reshape(part_count, capacity, pack.shape[1]),
        "dom",
        split_axis=0,
        concat_axis=0,
        tiled=True,
    ).reshape(slot_count, pack.shape[1])
    recv_scale = (
        pack_recv[:, columns].astype(jnp.float32) + pack_recv[:, columns + 1].astype(jnp.float32)
    ) + pack_recv[:, columns + 2].astype(jnp.float32)
    grad_recv = recv_scale[:, None] * pack_recv[:, :columns].astype(jnp.float32)
    rep_count = lax.axis_size("rep")
    neg_order = neg_grad.reshape(part_count // 8, 4, 2, rep_count, -1, columns)
    neg_order = neg_order.transpose(2, 3, 1, 0, 4, 5).reshape(-1, columns)
    orders = (("core", "x", "y", "z"), ("core", "y", "x", "z"))
    width = columns // len(orders)
    lanes = [(0, width * i, width, order, order[::-1]) for i, order in enumerate(orders)]
    lanes.append((1, 0, columns, ("core", "y", "x", "z"), ()))
    relation_flat, owned = lane_reduce([rel_stack.reshape(-1, columns), neg_order], lanes, 0)
    relation_grad = relation_flat.reshape(rel_stack.shape)
    neg_rows = owned.shape[0]
    neg_ids = lax.dynamic_slice_in_dim(neg_local, lax.axis_index("rep") * neg_rows, neg_rows)
    target_ids = jnp.concatenate([head_local, recv_ids.reshape(-1), neg_ids])
    target_rows = jnp.concatenate(
        [head_grad, grad_recv.reshape(slot_count, columns), owned], axis=0
    )
    block_rows = ent_dev
    block_count = ent_dev // block_rows

    def add_block(start):
        hot = (
            target_ids[None, :] == (start + jnp.arange(block_rows, dtype=jnp.int32))[:, None]
        ).astype(jnp.float32)
        return jnp.dot(
            hot, target_rows, precision=lax.Precision.HIGHEST, preferred_element_type=jnp.float32
        )

    local_grad = lax.map(add_block, jnp.arange(block_count, dtype=jnp.int32) * block_rows).reshape(
        ent_dev, columns
    )
    entity_grad = tree_reduce(local_grad, ("y",), ("y",), 2)
    return (entity_grad, relation_grad, edge_loss)


def solution(mesh):
    return jax.shard_map(
        local,
        mesh=mesh,
        in_specs=(
            P("dom", None),
            P(),
            P(("dom", "rep")),
            P(("dom", "rep")),
            P(("dom", "rep"), None),
            P(("dom", "rep")),
            P("dom"),
        ),
        out_specs=(P("dom", None), P(), P(("dom", "rep"))),
        check_vma=False,
    )
```

```python
import functools
import math

import jax
import jax.numpy as jnp
from jax import lax
from jax.experimental import pallas as pl
from jax.experimental.pallas import tpu as pltpu
from jax.sharding import PartitionSpec as P

D = 512


def _stage(name, dom, rep, n_dom, n_rep):
    core, xx, zz = dom % 2, (dom // 2) % 4, dom // 8
    if name == "core":
        return 2, core, lambda j: ((zz * 4 + xx) * 2 + j, rep)
    if name == "x":
        return min(4, n_dom // 2), xx, lambda j: ((zz * 4 + j) * 2 + core, rep)
    if name == "y":
        return n_rep, rep, lambda j: (dom, j)
    return max(1, n_dom // 8), zz, lambda j: ((j * 4 + xx) * 2 + core, rep)


def _sum_rows(parts, dst, rows):
    step = min(rows, 64)

    def body(i, carry):
        at = pl.ds(pl.multiple_of(i * step, 8), step)
        total = parts[0](at)
        for part in parts[1:]:
            total = total + part(at)
        dst[at, :] = total
        return carry

    lax.fori_loop(0, rows // step, body, 0)


def _reduce_kernel(rs, ag, sizes, x_ref, out_ref, *scratch):
    n_dom, n_rep = sizes
    dom = lax.axis_index("dom")
    rep = lax.axis_index("rep")
    mesh_id = pl.DeviceIdType.MESH
    rs_info = [_stage(n, dom, rep, n_dom, n_rep) for n in rs]
    ag_info = [_stage(n, dom, rep, n_dom, n_rep) for n in ag]
    nr = len(rs)
    recv_bufs = scratch[:nr]
    acc_bufs = scratch[nr : 2 * nr]
    full = scratch[2 * nr]
    rs_send, rs_recv, ag_send, ag_recv = scratch[2 * nr + 1 : 2 * nr + 5]

    barrier = pltpu.get_barrier_semaphore()
    greeted = 0
    seen = set()
    for name, (g, c, peer) in zip(list(rs) + list(ag), rs_info + ag_info):
        if name in seen:
            continue
        seen.add(name)
        for k in range(1, g):
            pl.semaphore_signal(barrier, 1, device_id=peer((c + k) % g), device_id_type=mesh_id)
            greeted += 1
    pl.semaphore_wait(barrier, greeted)

    sends = []
    src = x_ref
    length = x_ref.shape[0]
    base = 0
    si = 0
    for s, (g, c, peer) in enumerate(rs_info):
        piece = length // g
        for k in range(1, g):
            j = (c + k) % g
            cp = pltpu.make_async_remote_copy(
                src_ref=src.at[pl.ds(pl.multiple_of(j * piece, 8), piece)],
                dst_ref=recv_bufs[s].at[g - k - 1],
                send_sem=rs_send.at[si + k - 1],
                recv_sem=rs_recv.at[si + g - k - 1],
                device_id=peer(j),
                device_id_type=mesh_id,
            )
            cp.start()
            sends.append(cp)
        for k in range(1, g):
            j = (c + k) % g
            pltpu.make_async_remote_copy(
                src_ref=src.at[pl.ds(0, piece)],
                dst_ref=recv_bufs[s].at[k - 1],
                send_sem=rs_send.at[si + k - 1],
                recv_sem=rs_recv.at[si + k - 1],
                device_id=peer(j),
                device_id_type=mesh_id,
            ).wait_recv()
        own = pl.multiple_of(c * piece, 8)
        parts = [lambda at, src=src, own=own: src[pl.ds(own + at.start, at.size), :]]
        for k in range(1, g):
            parts.append(lambda at, b=recv_bufs[s], k=k: b[k - 1, at, :])
        _sum_rows(parts, acc_bufs[s], piece)
        src = acc_bufs[s]
        base = base + c * piece
        length = piece
        si += g - 1

    if not ag_info:
        out_ref[...] = src[...]
    else:
        full[pl.ds(pl.multiple_of(base, 8), length), :] = src[...]
        ai = 0
        for g, c, peer in ag_info:
            mine = pl.ds(pl.multiple_of(base, 8), length)
            for k in range(1, g):
                j = (c + k) % g
                cp = pltpu.make_async_remote_copy(
                    src_ref=full.at[mine],
                    dst_ref=full.at[mine],
                    send_sem=ag_send.at[ai + k - 1],
                    recv_sem=ag_recv.at[ai + g - k - 1],
                    device_id=peer(j),
                    device_id_type=mesh_id,
                )
                cp.start()
                sends.append(cp)
            start = base - c * length
            for k in range(1, g):
                j = (c + k) % g
                theirs = pl.ds(pl.multiple_of(start + j * length, 8), length)
                pltpu.make_async_remote_copy(
                    src_ref=full.at[theirs],
                    dst_ref=full.at[theirs],
                    send_sem=ag_send.at[ai + k - 1],
                    recv_sem=ag_recv.at[ai + k - 1],
                    device_id=peer(j),
                    device_id_type=mesh_id,
                ).wait_recv()
            base = start
            length = length * g
            ai += g - 1
        out_ref[...] = full[...]
    for cp in sends:
        cp.wait_send()


def tree_reduce(x, rs, ag, collective_id):
    n_dom = lax.axis_size("dom")
    n_rep = lax.axis_size("rep")
    rows, columns = x.shape
    shapes = []
    length = rows
    rs_sizes = []
    for name in rs:
        g = _stage(name, 0, 0, n_dom, n_rep)[0]
        rs_sizes.append(g)
    accs = []
    for g in rs_sizes:
        piece = length // g
        shapes.append(pltpu.VMEM((max(g - 1, 1), piece, columns), jnp.float32))
        accs.append(pltpu.VMEM((piece, columns), jnp.float32))
        length = piece
    n_ag = sum(_stage(name, 0, 0, n_dom, n_rep)[0] - 1 for name in ag)
    out_rows = rows if ag else length
    scratch = shapes + accs + [
        pltpu.VMEM((rows if ag else 8, columns), jnp.float32),
        pltpu.SemaphoreType.DMA((max(1, sum(g - 1 for g in rs_sizes)),)),
        pltpu.SemaphoreType.DMA((max(1, sum(g - 1 for g in rs_sizes)),)),
        pltpu.SemaphoreType.DMA((max(1, n_ag),)),
        pltpu.SemaphoreType.DMA((max(1, n_ag),)),
    ]
    return pl.pallas_call(
        functools.partial(_reduce_kernel, tuple(rs), tuple(ag), (n_dom, n_rep)),
        out_shape=jax.ShapeDtypeStruct((out_rows, columns), jnp.float32),
        in_specs=[pl.BlockSpec(memory_space=pltpu.VMEM)],
        out_specs=pl.BlockSpec(memory_space=pltpu.VMEM),
        scratch_shapes=scratch,
        compiler_params=pltpu.CompilerParams(
            collective_id=collective_id, has_side_effects=True, vmem_limit_bytes=60 * 1024 * 1024
        ),
        cost_estimate=pl.CostEstimate(
            flops=rows * columns * 2, transcendentals=0, bytes_accessed=rows * columns * 16
        ),
    )(x)


def _lane_kernel(lanes, sizes, n_in, *refs):
    n_dom, n_rep = sizes
    ins = refs[:n_in]
    outs = refs[n_in : 2 * n_in]
    scratch = refs[2 * n_in :]
    dom = lax.axis_index("dom")
    rep = lax.axis_index("rep")
    mesh_id = pl.DeviceIdType.MESH
    pos = 0
    lane_bufs = []
    for _, _, _, rs, _ in lanes:
        lane_bufs.append((scratch[pos : pos + len(rs)], scratch[pos + len(rs) : pos + 2 * len(rs)]))
        pos += 2 * len(rs)
    fulls = scratch[pos : pos + n_in]
    rs_send, rs_recv, ag_send, ag_recv = scratch[pos + n_in : pos + n_in + 4]

    def info(name):
        return _stage(name, dom, rep, n_dom, n_rep)

    barrier = pltpu.get_barrier_semaphore()
    greeted = 0
    names = []
    for lane in lanes:
        for name in lane[3] + lane[4]:
            if name not in names:
                names.append(name)
    for name in names:
        g, c, peer = info(name)
        for k in range(1, g):
            pl.semaphore_signal(barrier, 1, device_id=peer((c + k) % g), device_id_type=mesh_id)
            greeted += 1
    pl.semaphore_wait(barrier, greeted)

    sends = []
    state = [
        (ins[i], c0, w, ins[i].shape[0], 0) for i, c0, w, _, _ in lanes
    ]
    rs_base = []
    total = 0
    for lane in lanes:
        rs_base.append(total)
        total += sum(info(name)[0] - 1 for name in lane[3])
    for t in range(max(len(lane[3]) for lane in lanes)):
        pending = []
        offsets = [rs_base[li] + sum(info(n)[0] - 1 for n in lane[3][:t]) for li, lane in enumerate(lanes)]
        for li, lane in enumerate(lanes):
            if t >= len(lane[3]):
                continue
            g, c, peer = info(lane[3][t])
            ref, c0, w, length, gbase = state[li]
            piece = length // g
            si = offsets[li]
            recv = lane_bufs[li][0][t]
            for k in range(1, g):
                j = (c + k) % g
                cp = pltpu.make_async_remote_copy(
                    src_ref=ref.at[pl.ds(pl.multiple_of(j * piece, 8), piece), pl.ds(c0, w)],
                    dst_ref=recv.at[g - k - 1],
                    send_sem=rs_send.at[si + k - 1],
                    recv_sem=rs_recv.at[si + g - k - 1],
                    device_id=peer(j),
                    device_id_type=mesh_id,
                )
                cp.start()
                sends.append(cp)
            pending.append(li)
        for li in pending:
            lane = lanes[li]
            g, c, peer = info(lane[3][t])
            ref, c0, w, length, gbase = state[li]
            piece = length // g
            si = offsets[li]
            recv = lane_bufs[li][0][t]
            acc = lane_bufs[li][1][t]
            for k in range(1, g):
                j = (c + k) % g
                pltpu.make_async_remote_copy(
                    src_ref=ref.at[pl.ds(0, piece), pl.ds(c0, w)],
                    dst_ref=recv.at[k - 1],
                    send_sem=rs_send.at[si + k - 1],
                    recv_sem=rs_recv.at[si + k - 1],
                    device_id=peer(j),
                    device_id_type=mesh_id,
                ).wait_recv()
            own = pl.multiple_of(c * piece, 8)
            parts = [lambda at, ref=ref, own=own, c0=c0, w=w: ref[pl.ds(own + at.start, at.size), pl.ds(c0, w)]]
            for k in range(1, g):
                parts.append(lambda at, b=recv, k=k: b[k - 1, at, :])
            _sum_rows(parts, acc, piece)
            state[li] = (acc, 0, w, piece, gbase + c * piece)

    ag_state = []
    for li, lane in enumerate(lanes):
        acc, _, w, length, gbase = state[li]
        i, c0 = lane[0], lane[1]
        if lane[4]:
            fulls[i][pl.ds(pl.multiple_of(gbase, 8), length), pl.ds(c0, w)] = acc[...]
        else:
            outs[i][...] = acc[...]
        ag_state.append((length, gbase))
    ag_base = []
    total = 0
    for lane in lanes:
        ag_base.append(total)
        total += sum(info(name)[0] - 1 for name in lane[4])
    for t in range(max(len(lane[4]) for lane in lanes)):
        pending = []
        offsets = [ag_base[li] + sum(info(n)[0] - 1 for n in lane[4][:t]) for li, lane in enumerate(lanes)]
        for li, lane in enumerate(lanes):
            if t >= len(lane[4]):
                continue
            g, c, peer = info(lane[4][t])
            length, gbase = ag_state[li]
            full = fulls[lane[0]]
            cols = pl.ds(lane[1], lane[2])
            mine = pl.ds(pl.multiple_of(gbase, 8), length)
            ai = offsets[li]
            for k in range(1, g):
                j = (c + k) % g
                cp = pltpu.make_async_remote_copy(
                    src_ref=full.at[mine, cols],
                    dst_ref=full.at[mine, cols],
                    send_sem=ag_send.at[ai + k - 1],
                    recv_sem=ag_recv.at[ai + g - k - 1],
                    device_id=peer(j),
                    device_id_type=mesh_id,
                )
                cp.start()
                sends.append(cp)
            pending.append(li)
        for li in pending:
            lane = lanes[li]
            g, c, peer = info(lane[4][t])
            length, gbase = ag_state[li]
            full = fulls[lane[0]]
            cols = pl.ds(lane[1], lane[2])
            ai = offsets[li]
            start = gbase - c * length
            for k in range(1, g):
                j = (c + k) % g
                theirs = pl.ds(pl.multiple_of(start + j * length, 8), length)
                pltpu.make_async_remote_copy(
                    src_ref=full.at[theirs, cols],
                    dst_ref=full.at[theirs, cols],
                    send_sem=ag_send.at[ai + k - 1],
                    recv_sem=ag_recv.at[ai + k - 1],
                    device_id=peer(j),
                    device_id_type=mesh_id,
                ).wait_recv()
            ag_state[li] = (length * g, start)
    gathered = sorted({lane[0] for lane in lanes if lane[4]})
    for i in gathered:
        outs[i][...] = fulls[i][...]
    for cp in sends:
        cp.wait_send()


def lane_reduce(inputs, lanes, collective_id):
    n_dom = lax.axis_size("dom")
    n_rep = lax.axis_size("rep")
    scratch = []
    recv_shapes, acc_shapes = [], []
    n_rs = n_ag = 0
    out_shapes = [None] * len(inputs)
    for i, c0, w, rs, ag in lanes:
        length = inputs[i].shape[0]
        recv, accs = [], []
        for name in rs:
            g = _stage(name, 0, 0, n_dom, n_rep)[0]
            piece = length // g
            recv.append(pltpu.VMEM((max(g - 1, 1), piece, w), jnp.float32))
            accs.append(pltpu.VMEM((piece, w), jnp.float32))
            length = piece
            n_rs += g - 1
        n_ag += sum(_stage(name, 0, 0, n_dom, n_rep)[0] - 1 for name in ag)
        scratch += recv + accs
        out_shapes[i] = inputs[i].shape if ag else (length, w)
    for i, x in enumerate(inputs):
        scratch.append(pltpu.VMEM(x.shape if any(l[0] == i and l[4] for l in lanes) else (8, 128), jnp.float32))
    scratch += [
        pltpu.SemaphoreType.DMA((max(1, n_rs),)),
        pltpu.SemaphoreType.DMA((max(1, n_rs),)),
        pltpu.SemaphoreType.DMA((max(1, n_ag),)),
        pltpu.SemaphoreType.DMA((max(1, n_ag),)),
    ]
    moved = sum(x.size for x in inputs) * 4
    return pl.pallas_call(
        functools.partial(_lane_kernel, tuple(lanes), (n_dom, n_rep), len(inputs)),
        out_shape=[jax.ShapeDtypeStruct(shape, jnp.float32) for shape in out_shapes],
        in_specs=[pl.BlockSpec(memory_space=pltpu.VMEM)] * len(inputs),
        out_specs=[pl.BlockSpec(memory_space=pltpu.VMEM)] * len(inputs),
        scratch_shapes=scratch,
        compiler_params=pltpu.CompilerParams(
            collective_id=collective_id, has_side_effects=True, vmem_limit_bytes=62 * 1024 * 1024
        ),
        cost_estimate=pl.CostEstimate(flops=moved, transcendentals=0, bytes_accessed=moved * 4),
    )(*inputs)


def pick_rows(table, ids):
    hot = (ids[:, None] == jnp.arange(table.shape[0], dtype=ids.dtype)[None, :]).astype(table.dtype)
    return jnp.dot(hot, table, preferred_element_type=jnp.float32).astype(table.dtype)


def local(entities, relations, head_local, rel_ids, tail_part, tail_local, neg_local):
    factor = 1.0 / math.sqrt(D)
    ent_dev = entities.shape[0]
    columns = entities.shape[1]
    edge_count = head_local.shape[0]
    part_count = lax.axis_size("dom")
    capacity = 2 * edge_count // part_count
    slot_count = part_count * capacity
    relation_count = relations.shape[0]
    head_rows = pick_rows(entities, head_local)
    selectors = [(rel_ids == relation)[:, None] for relation in range(relation_count)]
    query_sum = jnp.zeros((edge_count, columns), jnp.float32)
    for relation in range(relation_count):
        picked = jnp.where(selectors[relation], head_rows, jnp.zeros_like(head_rows))
        query_sum = query_sum + jnp.dot(
            picked, relations[relation], preferred_element_type=jnp.float32
        )
    queries = query_sum.astype(jnp.bfloat16)
    target = tail_part[:, 0]
    target_hot = (target[:, None] == jnp.arange(part_count, dtype=jnp.int32)[None, :]).astype(
        jnp.int32
    )
    earlier = jnp.cumsum(target_hot, axis=0) - target_hot
    position = jnp.sum(earlier * target_hot, axis=1)
    slot_index = target * capacity + position
    slot_match = (slot_index[None, :] == jnp.arange(slot_count, dtype=jnp.int32)[:, None]).astype(
        jnp.int32
    )
    filled = jnp.sum(slot_match, axis=1) > 0
    source = jnp.sum(slot_match * jnp.arange(edge_count, dtype=jnp.int32)[None, :], axis=1)
    send_ids = jnp.sum(slot_match * tail_local[None, :], axis=1).reshape(part_count, capacity)
    recv_ids = lax.all_to_all(send_ids, "dom", split_axis=0, concat_axis=0, tiled=True)
    looked_up = pick_rows(entities, recv_ids.reshape(-1)).reshape(
        part_count, capacity, columns
    )
    returned = lax.all_to_all(looked_up, "dom", split_axis=0, concat_axis=0, tiled=True)
    tail_embed = pick_rows(returned.reshape(slot_count, columns), slot_index)
    own_negs = pick_rows(entities, neg_local)
    negatives = lax.all_gather(own_negs, "dom", axis=0, tiled=True)
    rep_count = lax.axis_size("rep")
    negatives = negatives.reshape(part_count // 8, 4, 2, rep_count, -1, columns)
    negatives = negatives.transpose(2, 3, 1, 0, 4, 5).reshape(-1, columns)
    positive = (
        jnp.sum(queries.astype(jnp.float32) * tail_embed.astype(jnp.float32), axis=1) * factor
    )
    scores = (
        lax.dot_general(
            queries, negatives, (((1,), (1,)), ((), ())), preferred_element_type=jnp.float32
        )
        * factor
    )
    row_max = jnp.maximum(positive, jnp.max(scores, axis=1))
    exp_pos = jnp.exp(positive - row_max)
    exp_neg = jnp.exp(scores - row_max[:, None])
    partition_sum = exp_pos + jnp.sum(exp_neg, axis=1)
    edge_loss = jnp.log(partition_sum) + row_max - positive
    prob_pos = exp_pos / partition_sum
    prob_neg = (exp_neg / partition_sum[:, None]).astype(jnp.bfloat16)
    mixed = jnp.dot(prob_neg, negatives, preferred_element_type=jnp.float32)
    query_grad = (
        factor * ((prob_pos - 1.0)[:, None] * tail_embed.astype(jnp.float32) + mixed)
    ).astype(jnp.bfloat16)
    tail_grad = factor * (prob_pos - 1.0)[:, None] * queries.astype(jnp.float32)
    head_grad = jnp.zeros((edge_count, columns), jnp.float32)
    rel_terms = []
    for relation in range(relation_count):
        picked_grad = jnp.where(selectors[relation], query_grad, jnp.zeros_like(query_grad))
        head_grad = head_grad + lax.dot_general(
            picked_grad,
            relations[relation],
            (((1,), (1,)), ((), ())),
            preferred_element_type=jnp.float32,
        )
        picked_rows = jnp.where(selectors[relation], head_rows, jnp.zeros_like(head_rows))
        rel_terms.append(
            lax.dot_general(
                picked_rows,
                query_grad,
                (((0,), (0,)), ((), ())),
                preferred_element_type=jnp.float32,
            )
        )
    rel_stack, prob_neg_late, queries_late = lax.optimization_barrier(
        (jnp.stack(rel_terms), prob_neg, queries)
    )
    neg_grad = factor * lax.dot_general(
        prob_neg_late, queries_late, (((0,), (0,)), ((), ())), preferred_element_type=jnp.float32
    )
    scale = factor * (prob_pos - 1.0)
    scale_hi = lax.reduce_precision(scale, exponent_bits=8, mantissa_bits=7)
    scale_rest = scale - scale_hi
    scale_mid = lax.reduce_precision(scale_rest, exponent_bits=8, mantissa_bits=7)
    scale_lo = scale_rest - scale_mid
    pack = jnp.concatenate(
        [
            queries,
            jnp.stack([scale_hi, scale_mid, scale_lo], axis=1).astype(jnp.bfloat16),
            jnp.zeros((edge_count, 125), jnp.bfloat16),
        ],
        axis=1,
    )
    pack_send = jnp.dot(
        slot_match.astype(jnp.bfloat16), pack, preferred_element_type=jnp.float32
    ).astype(jnp.bfloat16)
    pack_recv = lax.all_to_all(
        pack_send.reshape(part_count, capacity, pack.shape[1]),
        "dom",
        split_axis=0,
        concat_axis=0,
        tiled=True,
    ).reshape(slot_count, pack.shape[1])
    recv_scale = (
        pack_recv[:, columns].astype(jnp.float32) + pack_recv[:, columns + 1].astype(jnp.float32)
    ) + pack_recv[:, columns + 2].astype(jnp.float32)
    grad_recv = recv_scale[:, None] * pack_recv[:, :columns].astype(jnp.float32)
    rep_count = lax.axis_size("rep")
    neg_order = neg_grad
    orders = (("core", "x", "y", "z"), ("core", "y", "x", "z"))
    width = columns // len(orders)
    lanes = [(0, width * i, width, order, order[::-1]) for i, order in enumerate(orders)]
    lanes.append((1, 0, columns, ("core", "y", "x", "z"), ()))
    relation_flat, owned = lane_reduce([rel_stack.reshape(-1, columns), neg_order], lanes, 0)
    relation_grad = relation_flat.reshape(rel_stack.shape)
    neg_rows = owned.shape[0]
    neg_ids = lax.dynamic_slice_in_dim(neg_local, lax.axis_index("rep") * neg_rows, neg_rows)
    target_ids = jnp.concatenate([head_local, recv_ids.reshape(-1), neg_ids])
    target_rows = jnp.concatenate(
        [head_grad, grad_recv.reshape(slot_count, columns), owned], axis=0
    )
    block_rows = ent_dev
    block_count = ent_dev // block_rows

    def add_block(start):
        hot = (
            target_ids[None, :] == (start + jnp.arange(block_rows, dtype=jnp.int32))[:, None]
        ).astype(jnp.float32)
        return jnp.dot(
            hot, target_rows, precision=lax.Precision.HIGHEST, preferred_element_type=jnp.float32
        )

    local_grad = lax.map(add_block, jnp.arange(block_count, dtype=jnp.int32) * block_rows).reshape(
        ent_dev, columns
    )
    entity_grad = tree_reduce(local_grad, ("y",), ("y",), 2)
    return (entity_grad, relation_grad, edge_loss)


def solution(mesh):
    return jax.shard_map(
        local,
        mesh=mesh,
        in_specs=(
            P("dom", None),
            P(),
            P(("dom", "rep")),
            P(("dom", "rep")),
            P(("dom", "rep"), None),
            P(("dom", "rep")),
            P("dom"),
        ),
        out_specs=(P("dom", None), P(), P(("dom", "rep"))),
        check_vma=False,
    )
```

```python
import functools
import math

import jax
import jax.numpy as jnp
from jax import lax
from jax.experimental import pallas as pl
from jax.experimental.pallas import tpu as pltpu
from jax.sharding import PartitionSpec as P

D = 512


def _stage(name, dom, rep, n_dom, n_rep):
    core, xx, zz = dom % 2, (dom // 2) % 4, dom // 8
    if name == "core":
        return 2, core, lambda j: ((zz * 4 + xx) * 2 + j, rep)
    if name == "x":
        return min(4, n_dom // 2), xx, lambda j: ((zz * 4 + j) * 2 + core, rep)
    if name == "y":
        return n_rep, rep, lambda j: (dom, j)
    return max(1, n_dom // 8), zz, lambda j: ((j * 4 + xx) * 2 + core, rep)


def _sum_rows(parts, dst, rows):
    step = min(rows, 64)

    def body(i, carry):
        at = pl.ds(pl.multiple_of(i * step, 8), step)
        total = parts[0](at)
        for part in parts[1:]:
            total = total + part(at)
        dst[at, :] = total
        return carry

    lax.fori_loop(0, rows // step, body, 0)


def _reduce_kernel(rs, ag, sizes, x_ref, out_ref, *scratch):
    n_dom, n_rep = sizes
    dom = lax.axis_index("dom")
    rep = lax.axis_index("rep")
    mesh_id = pl.DeviceIdType.MESH
    rs_info = [_stage(n, dom, rep, n_dom, n_rep) for n in rs]
    ag_info = [_stage(n, dom, rep, n_dom, n_rep) for n in ag]
    nr = len(rs)
    recv_bufs = scratch[:nr]
    acc_bufs = scratch[nr : 2 * nr]
    full = scratch[2 * nr]
    rs_send, rs_recv, ag_send, ag_recv = scratch[2 * nr + 1 : 2 * nr + 5]

    barrier = pltpu.get_barrier_semaphore()
    greeted = 0
    seen = set()
    for name, (g, c, peer) in zip(list(rs) + list(ag), rs_info + ag_info):
        if name in seen:
            continue
        seen.add(name)
        for k in range(1, g):
            pl.semaphore_signal(barrier, 1, device_id=peer((c + k) % g), device_id_type=mesh_id)
            greeted += 1
    pl.semaphore_wait(barrier, greeted)

    sends = []
    src = x_ref
    length = x_ref.shape[0]
    base = 0
    si = 0
    for s, (g, c, peer) in enumerate(rs_info):
        piece = length // g
        for k in range(1, g):
            j = (c + k) % g
            cp = pltpu.make_async_remote_copy(
                src_ref=src.at[pl.ds(pl.multiple_of(j * piece, 8), piece)],
                dst_ref=recv_bufs[s].at[g - k - 1],
                send_sem=rs_send.at[si + k - 1],
                recv_sem=rs_recv.at[si + g - k - 1],
                device_id=peer(j),
                device_id_type=mesh_id,
            )
            cp.start()
            sends.append(cp)
        for k in range(1, g):
            j = (c + k) % g
            pltpu.make_async_remote_copy(
                src_ref=src.at[pl.ds(0, piece)],
                dst_ref=recv_bufs[s].at[k - 1],
                send_sem=rs_send.at[si + k - 1],
                recv_sem=rs_recv.at[si + k - 1],
                device_id=peer(j),
                device_id_type=mesh_id,
            ).wait_recv()
        own = pl.multiple_of(c * piece, 8)
        parts = [lambda at, src=src, own=own: src[pl.ds(own + at.start, at.size), :]]
        for k in range(1, g):
            parts.append(lambda at, b=recv_bufs[s], k=k: b[k - 1, at, :])
        _sum_rows(parts, acc_bufs[s], piece)
        src = acc_bufs[s]
        base = base + c * piece
        length = piece
        si += g - 1

    if not ag_info:
        out_ref[...] = src[...]
    else:
        full[pl.ds(pl.multiple_of(base, 8), length), :] = src[...]
        ai = 0
        for g, c, peer in ag_info:
            mine = pl.ds(pl.multiple_of(base, 8), length)
            for k in range(1, g):
                j = (c + k) % g
                cp = pltpu.make_async_remote_copy(
                    src_ref=full.at[mine],
                    dst_ref=full.at[mine],
                    send_sem=ag_send.at[ai + k - 1],
                    recv_sem=ag_recv.at[ai + g - k - 1],
                    device_id=peer(j),
                    device_id_type=mesh_id,
                )
                cp.start()
                sends.append(cp)
            start = base - c * length
            for k in range(1, g):
                j = (c + k) % g
                theirs = pl.ds(pl.multiple_of(start + j * length, 8), length)
                pltpu.make_async_remote_copy(
                    src_ref=full.at[theirs],
                    dst_ref=full.at[theirs],
                    send_sem=ag_send.at[ai + k - 1],
                    recv_sem=ag_recv.at[ai + k - 1],
                    device_id=peer(j),
                    device_id_type=mesh_id,
                ).wait_recv()
            base = start
            length = length * g
            ai += g - 1
        out_ref[...] = full[...]
    for cp in sends:
        cp.wait_send()


def tree_reduce(x, rs, ag, collective_id):
    n_dom = lax.axis_size("dom")
    n_rep = lax.axis_size("rep")
    rows, columns = x.shape
    shapes = []
    length = rows
    rs_sizes = []
    for name in rs:
        g = _stage(name, 0, 0, n_dom, n_rep)[0]
        rs_sizes.append(g)
    accs = []
    for g in rs_sizes:
        piece = length // g
        shapes.append(pltpu.VMEM((max(g - 1, 1), piece, columns), jnp.float32))
        accs.append(pltpu.VMEM((piece, columns), jnp.float32))
        length = piece
    n_ag = sum(_stage(name, 0, 0, n_dom, n_rep)[0] - 1 for name in ag)
    out_rows = rows if ag else length
    scratch = shapes + accs + [
        pltpu.VMEM((rows if ag else 8, columns), jnp.float32),
        pltpu.SemaphoreType.DMA((max(1, sum(g - 1 for g in rs_sizes)),)),
        pltpu.SemaphoreType.DMA((max(1, sum(g - 1 for g in rs_sizes)),)),
        pltpu.SemaphoreType.DMA((max(1, n_ag),)),
        pltpu.SemaphoreType.DMA((max(1, n_ag),)),
    ]
    return pl.pallas_call(
        functools.partial(_reduce_kernel, tuple(rs), tuple(ag), (n_dom, n_rep)),
        out_shape=jax.ShapeDtypeStruct((out_rows, columns), jnp.float32),
        in_specs=[pl.BlockSpec(memory_space=pltpu.VMEM)],
        out_specs=pl.BlockSpec(memory_space=pltpu.VMEM),
        scratch_shapes=scratch,
        compiler_params=pltpu.CompilerParams(
            collective_id=collective_id, has_side_effects=True, vmem_limit_bytes=60 * 1024 * 1024
        ),
        cost_estimate=pl.CostEstimate(
            flops=rows * columns * 2, transcendentals=0, bytes_accessed=rows * columns * 16
        ),
    )(x)


def _lane_kernel(lanes, sizes, n_in, *refs):
    n_dom, n_rep = sizes
    ins = refs[:n_in]
    outs = refs[n_in : 2 * n_in]
    scratch = refs[2 * n_in :]
    dom = lax.axis_index("dom")
    rep = lax.axis_index("rep")
    mesh_id = pl.DeviceIdType.MESH
    pos = 0
    lane_bufs = []
    for _, _, _, rs, _ in lanes:
        lane_bufs.append((scratch[pos : pos + len(rs)], scratch[pos + len(rs) : pos + 2 * len(rs)]))
        pos += 2 * len(rs)
    fulls = scratch[pos : pos + n_in]
    rs_send, rs_recv, ag_send, ag_recv = scratch[pos + n_in : pos + n_in + 4]

    def info(name):
        return _stage(name, dom, rep, n_dom, n_rep)

    barrier = pltpu.get_barrier_semaphore()
    greeted = 0
    names = []
    for lane in lanes:
        for name in lane[3] + lane[4]:
            if name not in names:
                names.append(name)
    for name in names:
        g, c, peer = info(name)
        for k in range(1, g):
            pl.semaphore_signal(barrier, 1, device_id=peer((c + k) % g), device_id_type=mesh_id)
            greeted += 1
    pl.semaphore_wait(barrier, greeted)

    sends = []
    state = [
        (ins[i], c0, w, ins[i].shape[0], 0) for i, c0, w, _, _ in lanes
    ]
    rs_base = []
    total = 0
    for lane in lanes:
        rs_base.append(total)
        total += sum(info(name)[0] - 1 for name in lane[3])
    for t in range(max(len(lane[3]) for lane in lanes)):
        pending = []
        offsets = [rs_base[li] + sum(info(n)[0] - 1 for n in lane[3][:t]) for li, lane in enumerate(lanes)]
        for li, lane in enumerate(lanes):
            if t >= len(lane[3]):
                continue
            g, c, peer = info(lane[3][t])
            ref, c0, w, length, gbase = state[li]
            piece = length // g
            si = offsets[li]
            recv = lane_bufs[li][0][t]
            for k in range(1, g):
                j = (c + k) % g
                cp = pltpu.make_async_remote_copy(
                    src_ref=ref.at[pl.ds(pl.multiple_of(j * piece, 8), piece), pl.ds(c0, w)],
                    dst_ref=recv.at[g - k - 1],
                    send_sem=rs_send.at[si + k - 1],
                    recv_sem=rs_recv.at[si + g - k - 1],
                    device_id=peer(j),
                    device_id_type=mesh_id,
                )
                cp.start()
                sends.append(cp)
            pending.append(li)
        for li in pending:
            lane = lanes[li]
            g, c, peer = info(lane[3][t])
            ref, c0, w, length, gbase = state[li]
            piece = length // g
            si = offsets[li]
            recv = lane_bufs[li][0][t]
            acc = lane_bufs[li][1][t]
            for k in range(1, g):
                j = (c + k) % g
                pltpu.make_async_remote_copy(
                    src_ref=ref.at[pl.ds(0, piece), pl.ds(c0, w)],
                    dst_ref=recv.at[k - 1],
                    send_sem=rs_send.at[si + k - 1],
                    recv_sem=rs_recv.at[si + k - 1],
                    device_id=peer(j),
                    device_id_type=mesh_id,
                ).wait_recv()
            own = pl.multiple_of(c * piece, 8)
            parts = [lambda at, ref=ref, own=own, c0=c0, w=w: ref[pl.ds(own + at.start, at.size), pl.ds(c0, w)]]
            for k in range(1, g):
                parts.append(lambda at, b=recv, k=k: b[k - 1, at, :])
            _sum_rows(parts, acc, piece)
            state[li] = (acc, 0, w, piece, gbase + c * piece)

    ag_state = []
    for li, lane in enumerate(lanes):
        acc, _, w, length, gbase = state[li]
        i, c0 = lane[0], lane[1]
        if lane[4]:
            fulls[i][pl.ds(pl.multiple_of(gbase, 8), length), pl.ds(c0, w)] = acc[...]
        else:
            outs[i][...] = acc[...]
        ag_state.append((length, gbase))
    ag_base = []
    total = 0
    for lane in lanes:
        ag_base.append(total)
        total += sum(info(name)[0] - 1 for name in lane[4])
    for t in range(max(len(lane[4]) for lane in lanes)):
        pending = []
        offsets = [ag_base[li] + sum(info(n)[0] - 1 for n in lane[4][:t]) for li, lane in enumerate(lanes)]
        for li, lane in enumerate(lanes):
            if t >= len(lane[4]):
                continue
            g, c, peer = info(lane[4][t])
            length, gbase = ag_state[li]
            full = fulls[lane[0]]
            cols = pl.ds(lane[1], lane[2])
            mine = pl.ds(pl.multiple_of(gbase, 8), length)
            ai = offsets[li]
            for k in range(1, g):
                j = (c + k) % g
                cp = pltpu.make_async_remote_copy(
                    src_ref=full.at[mine, cols],
                    dst_ref=full.at[mine, cols],
                    send_sem=ag_send.at[ai + k - 1],
                    recv_sem=ag_recv.at[ai + g - k - 1],
                    device_id=peer(j),
                    device_id_type=mesh_id,
                )
                cp.start()
                sends.append(cp)
            pending.append(li)
        for li in pending:
            lane = lanes[li]
            g, c, peer = info(lane[4][t])
            length, gbase = ag_state[li]
            full = fulls[lane[0]]
            cols = pl.ds(lane[1], lane[2])
            ai = offsets[li]
            start = gbase - c * length
            for k in range(1, g):
                j = (c + k) % g
                theirs = pl.ds(pl.multiple_of(start + j * length, 8), length)
                pltpu.make_async_remote_copy(
                    src_ref=full.at[theirs, cols],
                    dst_ref=full.at[theirs, cols],
                    send_sem=ag_send.at[ai + k - 1],
                    recv_sem=ag_recv.at[ai + k - 1],
                    device_id=peer(j),
                    device_id_type=mesh_id,
                ).wait_recv()
            ag_state[li] = (length * g, start)
    gathered = sorted({lane[0] for lane in lanes if lane[4]})
    for i in gathered:
        outs[i][...] = fulls[i][...]
    for cp in sends:
        cp.wait_send()


def lane_reduce(inputs, lanes, collective_id):
    n_dom = lax.axis_size("dom")
    n_rep = lax.axis_size("rep")
    scratch = []
    recv_shapes, acc_shapes = [], []
    n_rs = n_ag = 0
    out_shapes = [None] * len(inputs)
    for i, c0, w, rs, ag in lanes:
        length = inputs[i].shape[0]
        recv, accs = [], []
        for name in rs:
            g = _stage(name, 0, 0, n_dom, n_rep)[0]
            piece = length // g
            recv.append(pltpu.VMEM((max(g - 1, 1), piece, w), jnp.float32))
            accs.append(pltpu.VMEM((piece, w), jnp.float32))
            length = piece
            n_rs += g - 1
        n_ag += sum(_stage(name, 0, 0, n_dom, n_rep)[0] - 1 for name in ag)
        scratch += recv + accs
        out_shapes[i] = inputs[i].shape if ag else (length, w)
    for i, x in enumerate(inputs):
        scratch.append(pltpu.VMEM(x.shape if any(l[0] == i and l[4] for l in lanes) else (8, 128), jnp.float32))
    scratch += [
        pltpu.SemaphoreType.DMA((max(1, n_rs),)),
        pltpu.SemaphoreType.DMA((max(1, n_rs),)),
        pltpu.SemaphoreType.DMA((max(1, n_ag),)),
        pltpu.SemaphoreType.DMA((max(1, n_ag),)),
    ]
    moved = sum(x.size for x in inputs) * 4
    return pl.pallas_call(
        functools.partial(_lane_kernel, tuple(lanes), (n_dom, n_rep), len(inputs)),
        out_shape=[jax.ShapeDtypeStruct(shape, jnp.float32) for shape in out_shapes],
        in_specs=[pl.BlockSpec(memory_space=pltpu.VMEM)] * len(inputs),
        out_specs=[pl.BlockSpec(memory_space=pltpu.VMEM)] * len(inputs),
        scratch_shapes=scratch,
        compiler_params=pltpu.CompilerParams(
            collective_id=collective_id, has_side_effects=True, vmem_limit_bytes=62 * 1024 * 1024
        ),
        cost_estimate=pl.CostEstimate(flops=moved, transcendentals=0, bytes_accessed=moved * 4),
    )(*inputs)


def pick_rows(table, ids):
    hot = (ids[:, None] == jnp.arange(table.shape[0], dtype=ids.dtype)[None, :]).astype(table.dtype)
    return jnp.dot(hot, table, preferred_element_type=jnp.float32).astype(table.dtype)


def local(entities, relations, head_local, rel_ids, tail_part, tail_local, neg_local):
    factor = 1.0 / math.sqrt(D)
    ent_dev = entities.shape[0]
    columns = entities.shape[1]
    edge_count = head_local.shape[0]
    part_count = lax.axis_size("dom")
    capacity = 2 * edge_count // part_count
    slot_count = part_count * capacity
    relation_count = relations.shape[0]
    head_rows = pick_rows(entities, head_local)
    selectors = [(rel_ids == relation)[:, None] for relation in range(relation_count)]
    query_sum = jnp.zeros((edge_count, columns), jnp.float32)
    for relation in range(relation_count):
        picked = jnp.where(selectors[relation], head_rows, jnp.zeros_like(head_rows))
        query_sum = query_sum + jnp.dot(
            picked, relations[relation], preferred_element_type=jnp.float32
        )
    queries = query_sum.astype(jnp.bfloat16)
    target = tail_part[:, 0]
    target_hot = (target[:, None] == jnp.arange(part_count, dtype=jnp.int32)[None, :]).astype(
        jnp.int32
    )
    earlier = jnp.cumsum(target_hot, axis=0) - target_hot
    position = jnp.sum(earlier * target_hot, axis=1)
    slot_index = target * capacity + position
    slot_match = (slot_index[None, :] == jnp.arange(slot_count, dtype=jnp.int32)[:, None]).astype(
        jnp.int32
    )
    filled = jnp.sum(slot_match, axis=1) > 0
    source = jnp.sum(slot_match * jnp.arange(edge_count, dtype=jnp.int32)[None, :], axis=1)
    send_ids = jnp.sum(slot_match * tail_local[None, :], axis=1).reshape(part_count, capacity)
    recv_ids = lax.all_to_all(send_ids, "dom", split_axis=0, concat_axis=0, tiled=True)
    looked_up = pick_rows(entities, recv_ids.reshape(-1)).reshape(
        part_count, capacity, columns
    )
    returned = lax.all_to_all(looked_up, "dom", split_axis=0, concat_axis=0, tiled=True)
    tail_embed = pick_rows(returned.reshape(slot_count, columns), slot_index)
    own_negs = pick_rows(entities, neg_local)
    negatives = lax.all_gather(own_negs, "dom", axis=0, tiled=True)
    positive = (
        jnp.sum(queries.astype(jnp.float32) * tail_embed.astype(jnp.float32), axis=1) * factor
    )
    scores = (
        lax.dot_general(
            queries, negatives, (((1,), (1,)), ((), ())), preferred_element_type=jnp.float32
        )
        * factor
    )
    row_max = jnp.maximum(positive, jnp.max(scores, axis=1))
    exp_pos = jnp.exp(positive - row_max)
    exp_neg = jnp.exp(scores - row_max[:, None])
    partition_sum = exp_pos + jnp.sum(exp_neg, axis=1)
    edge_loss = jnp.log(partition_sum) + row_max - positive
    prob_pos = exp_pos / partition_sum
    prob_neg = (exp_neg / partition_sum[:, None]).astype(jnp.bfloat16)
    mixed = jnp.dot(prob_neg, negatives, preferred_element_type=jnp.float32)
    query_grad = (
        factor * ((prob_pos - 1.0)[:, None] * tail_embed.astype(jnp.float32) + mixed)
    ).astype(jnp.bfloat16)
    tail_grad = factor * (prob_pos - 1.0)[:, None] * queries.astype(jnp.float32)
    head_grad = jnp.zeros((edge_count, columns), jnp.float32)
    rel_terms = []
    for relation in range(relation_count):
        picked_grad = jnp.where(selectors[relation], query_grad, jnp.zeros_like(query_grad))
        head_grad = head_grad + lax.dot_general(
            picked_grad,
            relations[relation],
            (((1,), (1,)), ((), ())),
            preferred_element_type=jnp.float32,
        )
        picked_rows = jnp.where(selectors[relation], head_rows, jnp.zeros_like(head_rows))
        rel_terms.append(
            lax.dot_general(
                picked_rows,
                query_grad,
                (((0,), (0,)), ((), ())),
                preferred_element_type=jnp.float32,
            )
        )
    rel_stack, prob_neg_late, queries_late = lax.optimization_barrier(
        (jnp.stack(rel_terms), prob_neg, queries)
    )
    neg_grad = factor * lax.dot_general(
        prob_neg_late, queries_late, (((0,), (0,)), ((), ())), preferred_element_type=jnp.float32
    )
    scale = factor * (prob_pos - 1.0)
    scale_hi = lax.reduce_precision(scale, exponent_bits=8, mantissa_bits=7)
    scale_rest = scale - scale_hi
    scale_mid = lax.reduce_precision(scale_rest, exponent_bits=8, mantissa_bits=7)
    scale_lo = scale_rest - scale_mid
    pack = jnp.concatenate(
        [
            queries,
            jnp.stack([scale_hi, scale_mid, scale_lo], axis=1).astype(jnp.bfloat16),
            jnp.zeros((edge_count, 125), jnp.bfloat16),
        ],
        axis=1,
    )
    pack_send = jnp.dot(
        slot_match.astype(jnp.bfloat16), pack, preferred_element_type=jnp.float32
    ).astype(jnp.bfloat16)
    pack_recv = lax.all_to_all(
        pack_send.reshape(part_count, capacity, pack.shape[1]),
        "dom",
        split_axis=0,
        concat_axis=0,
        tiled=True,
    ).reshape(slot_count, pack.shape[1])
    recv_scale = (
        pack_recv[:, columns].astype(jnp.float32) + pack_recv[:, columns + 1].astype(jnp.float32)
    ) + pack_recv[:, columns + 2].astype(jnp.float32)
    grad_recv = recv_scale[:, None] * pack_recv[:, :columns].astype(jnp.float32)
    rep_count = lax.axis_size("rep")
    neg_order = neg_grad.reshape(part_count // 8, 4, 2, rep_count, -1, columns)
    neg_order = neg_order.transpose(2, 3, 1, 0, 4, 5).reshape(-1, columns)
    orders = (("core", "x", "y", "z"), ("core", "y", "x", "z"))
    width = columns // len(orders)
    lanes = [(0, width * i, width, order, order[::-1]) for i, order in enumerate(orders)]
    lanes.append((1, 0, columns, ("core", "y", "x", "z"), ()))
    relation_flat, owned = lane_reduce([rel_stack.reshape(-1, columns), neg_order], lanes, 0)
    relation_grad = relation_flat.reshape(rel_stack.shape)
    neg_rows = owned.shape[0]
    neg_ids = lax.dynamic_slice_in_dim(neg_local, lax.axis_index("rep") * neg_rows, neg_rows)
    target_ids = jnp.concatenate([head_local, recv_ids.reshape(-1), neg_ids])
    target_rows = jnp.concatenate(
        [head_grad, pack_recv[:, :columns].astype(jnp.float32), owned], axis=0
    )
    target_weights = jnp.concatenate(
        [jnp.ones((edge_count,), jnp.float32), recv_scale, jnp.ones((owned.shape[0],), jnp.float32)]
    )
    block_rows = ent_dev
    block_count = ent_dev // block_rows

    def add_block(start):
        hot = (
            target_ids[None, :] == (start + jnp.arange(block_rows, dtype=jnp.int32))[:, None]
        ).astype(jnp.float32) * target_weights[None, :]
        return jnp.dot(
            hot, target_rows, precision=lax.Precision.HIGHEST, preferred_element_type=jnp.float32
        )

    local_grad = lax.map(add_block, jnp.arange(block_count, dtype=jnp.int32) * block_rows).reshape(
        ent_dev, columns
    )
    entity_grad = tree_reduce(local_grad, ("y",), ("y",), 2)
    return (entity_grad, relation_grad, edge_loss)


def solution(mesh):
    return jax.shard_map(
        local,
        mesh=mesh,
        in_specs=(
            P("dom", None),
            P(),
            P(("dom", "rep")),
            P(("dom", "rep")),
            P(("dom", "rep"), None),
            P(("dom", "rep")),
            P("dom"),
        ),
        out_specs=(P("dom", None), P(), P(("dom", "rep"))),
        check_vma=False,
    )
```

```python
import functools
import math

import jax
import jax.numpy as jnp
from jax import lax
from jax.experimental import pallas as pl
from jax.experimental.pallas import tpu as pltpu
from jax.sharding import PartitionSpec as P

D = 512


def _stage(name, dom, rep, n_dom, n_rep):
    core, xx, zz = dom % 2, (dom // 2) % 4, dom // 8
    if name == "core":
        return 2, core, lambda j: ((zz * 4 + xx) * 2 + j, rep)
    if name == "x":
        return min(4, n_dom // 2), xx, lambda j: ((zz * 4 + j) * 2 + core, rep)
    if name == "y":
        return n_rep, rep, lambda j: (dom, j)
    return max(1, n_dom // 8), zz, lambda j: ((j * 4 + xx) * 2 + core, rep)


def _sum_rows(parts, dst, rows):
    step = min(rows, 64)

    def body(i, carry):
        at = pl.ds(pl.multiple_of(i * step, 8), step)
        total = parts[0](at)
        for part in parts[1:]:
            total = total + part(at)
        dst[at, :] = total
        return carry

    lax.fori_loop(0, rows // step, body, 0)


def _reduce_kernel(rs, ag, sizes, x_ref, out_ref, *scratch):
    n_dom, n_rep = sizes
    dom = lax.axis_index("dom")
    rep = lax.axis_index("rep")
    mesh_id = pl.DeviceIdType.MESH
    rs_info = [_stage(n, dom, rep, n_dom, n_rep) for n in rs]
    ag_info = [_stage(n, dom, rep, n_dom, n_rep) for n in ag]
    nr = len(rs)
    recv_bufs = scratch[:nr]
    acc_bufs = scratch[nr : 2 * nr]
    full = scratch[2 * nr]
    rs_send, rs_recv, ag_send, ag_recv = scratch[2 * nr + 1 : 2 * nr + 5]

    barrier = pltpu.get_barrier_semaphore()
    greeted = 0
    seen = set()
    for name, (g, c, peer) in zip(list(rs) + list(ag), rs_info + ag_info):
        if name in seen:
            continue
        seen.add(name)
        for k in range(1, g):
            pl.semaphore_signal(barrier, 1, device_id=peer((c + k) % g), device_id_type=mesh_id)
            greeted += 1
    pl.semaphore_wait(barrier, greeted)

    sends = []
    src = x_ref
    length = x_ref.shape[0]
    base = 0
    si = 0
    for s, (g, c, peer) in enumerate(rs_info):
        piece = length // g
        for k in range(1, g):
            j = (c + k) % g
            cp = pltpu.make_async_remote_copy(
                src_ref=src.at[pl.ds(pl.multiple_of(j * piece, 8), piece)],
                dst_ref=recv_bufs[s].at[g - k - 1],
                send_sem=rs_send.at[si + k - 1],
                recv_sem=rs_recv.at[si + g - k - 1],
                device_id=peer(j),
                device_id_type=mesh_id,
            )
            cp.start()
            sends.append(cp)
        for k in range(1, g):
            j = (c + k) % g
            pltpu.make_async_remote_copy(
                src_ref=src.at[pl.ds(0, piece)],
                dst_ref=recv_bufs[s].at[k - 1],
                send_sem=rs_send.at[si + k - 1],
                recv_sem=rs_recv.at[si + k - 1],
                device_id=peer(j),
                device_id_type=mesh_id,
            ).wait_recv()
        own = pl.multiple_of(c * piece, 8)
        parts = [lambda at, src=src, own=own: src[pl.ds(own + at.start, at.size), :]]
        for k in range(1, g):
            parts.append(lambda at, b=recv_bufs[s], k=k: b[k - 1, at, :])
        _sum_rows(parts, acc_bufs[s], piece)
        src = acc_bufs[s]
        base = base + c * piece
        length = piece
        si += g - 1

    if not ag_info:
        out_ref[...] = src[...]
    else:
        full[pl.ds(pl.multiple_of(base, 8), length), :] = src[...]
        ai = 0
        for g, c, peer in ag_info:
            mine = pl.ds(pl.multiple_of(base, 8), length)
            for k in range(1, g):
                j = (c + k) % g
                cp = pltpu.make_async_remote_copy(
                    src_ref=full.at[mine],
                    dst_ref=full.at[mine],
                    send_sem=ag_send.at[ai + k - 1],
                    recv_sem=ag_recv.at[ai + g - k - 1],
                    device_id=peer(j),
                    device_id_type=mesh_id,
                )
                cp.start()
                sends.append(cp)
            start = base - c * length
            for k in range(1, g):
                j = (c + k) % g
                theirs = pl.ds(pl.multiple_of(start + j * length, 8), length)
                pltpu.make_async_remote_copy(
                    src_ref=full.at[theirs],
                    dst_ref=full.at[theirs],
                    send_sem=ag_send.at[ai + k - 1],
                    recv_sem=ag_recv.at[ai + k - 1],
                    device_id=peer(j),
                    device_id_type=mesh_id,
                ).wait_recv()
            base = start
            length = length * g
            ai += g - 1
        out_ref[...] = full[...]
    for cp in sends:
        cp.wait_send()


def tree_reduce(x, rs, ag, collective_id):
    n_dom = lax.axis_size("dom")
    n_rep = lax.axis_size("rep")
    rows, columns = x.shape
    shapes = []
    length = rows
    rs_sizes = []
    for name in rs:
        g = _stage(name, 0, 0, n_dom, n_rep)[0]
        rs_sizes.append(g)
    accs = []
    for g in rs_sizes:
        piece = length // g
        shapes.append(pltpu.VMEM((max(g - 1, 1), piece, columns), jnp.float32))
        accs.append(pltpu.VMEM((piece, columns), jnp.float32))
        length = piece
    n_ag = sum(_stage(name, 0, 0, n_dom, n_rep)[0] - 1 for name in ag)
    out_rows = rows if ag else length
    scratch = shapes + accs + [
        pltpu.VMEM((rows if ag else 8, columns), jnp.float32),
        pltpu.SemaphoreType.DMA((max(1, sum(g - 1 for g in rs_sizes)),)),
        pltpu.SemaphoreType.DMA((max(1, sum(g - 1 for g in rs_sizes)),)),
        pltpu.SemaphoreType.DMA((max(1, n_ag),)),
        pltpu.SemaphoreType.DMA((max(1, n_ag),)),
    ]
    return pl.pallas_call(
        functools.partial(_reduce_kernel, tuple(rs), tuple(ag), (n_dom, n_rep)),
        out_shape=jax.ShapeDtypeStruct((out_rows, columns), jnp.float32),
        in_specs=[pl.BlockSpec(memory_space=pltpu.VMEM)],
        out_specs=pl.BlockSpec(memory_space=pltpu.VMEM),
        scratch_shapes=scratch,
        compiler_params=pltpu.CompilerParams(
            collective_id=collective_id, has_side_effects=True, vmem_limit_bytes=60 * 1024 * 1024
        ),
        cost_estimate=pl.CostEstimate(
            flops=rows * columns * 2, transcendentals=0, bytes_accessed=rows * columns * 16
        ),
    )(x)


def _lane_kernel(lanes, sizes, n_in, *refs):
    n_dom, n_rep = sizes
    ins = refs[:n_in]
    outs = refs[n_in : 2 * n_in]
    scratch = refs[2 * n_in :]
    dom = lax.axis_index("dom")
    rep = lax.axis_index("rep")
    mesh_id = pl.DeviceIdType.MESH
    pos = 0
    lane_bufs = []
    for _, _, _, rs, _ in lanes:
        lane_bufs.append((scratch[pos : pos + len(rs)], scratch[pos + len(rs) : pos + 2 * len(rs)]))
        pos += 2 * len(rs)
    fulls = scratch[pos : pos + n_in]
    rs_send, rs_recv, ag_send, ag_recv = scratch[pos + n_in : pos + n_in + 4]

    def info(name):
        return _stage(name, dom, rep, n_dom, n_rep)

    barrier = pltpu.get_barrier_semaphore()
    greeted = 0
    names = []
    for lane in lanes:
        for name in lane[3] + lane[4]:
            if name not in names:
                names.append(name)
    for name in names:
        g, c, peer = info(name)
        for k in range(1, g):
            pl.semaphore_signal(barrier, 1, device_id=peer((c + k) % g), device_id_type=mesh_id)
            greeted += 1
    pl.semaphore_wait(barrier, greeted)

    sends = []
    state = [
        (ins[i], c0, w, ins[i].shape[0], 0) for i, c0, w, _, _ in lanes
    ]
    rs_base = []
    total = 0
    for lane in lanes:
        rs_base.append(total)
        total += sum(info(name)[0] - 1 for name in lane[3])
    for t in range(max(len(lane[3]) for lane in lanes)):
        pending = []
        offsets = [rs_base[li] + sum(info(n)[0] - 1 for n in lane[3][:t]) for li, lane in enumerate(lanes)]
        for li, lane in enumerate(lanes):
            if t >= len(lane[3]):
                continue
            g, c, peer = info(lane[3][t])
            ref, c0, w, length, gbase = state[li]
            piece = length // g
            si = offsets[li]
            recv = lane_bufs[li][0][t]
            for k in range(1, g):
                j = (c + k) % g
                cp = pltpu.make_async_remote_copy(
                    src_ref=ref.at[pl.ds(pl.multiple_of(j * piece, 8), piece), pl.ds(c0, w)],
                    dst_ref=recv.at[g - k - 1],
                    send_sem=rs_send.at[si + k - 1],
                    recv_sem=rs_recv.at[si + g - k - 1],
                    device_id=peer(j),
                    device_id_type=mesh_id,
                )
                cp.start()
                sends.append(cp)
            pending.append(li)
        for li in pending:
            lane = lanes[li]
            g, c, peer = info(lane[3][t])
            ref, c0, w, length, gbase = state[li]
            piece = length // g
            si = offsets[li]
            recv = lane_bufs[li][0][t]
            acc = lane_bufs[li][1][t]
            for k in range(1, g):
                j = (c + k) % g
                pltpu.make_async_remote_copy(
                    src_ref=ref.at[pl.ds(0, piece), pl.ds(c0, w)],
                    dst_ref=recv.at[k - 1],
                    send_sem=rs_send.at[si + k - 1],
                    recv_sem=rs_recv.at[si + k - 1],
                    device_id=peer(j),
                    device_id_type=mesh_id,
                ).wait_recv()
            own = pl.multiple_of(c * piece, 8)
            parts = [lambda at, ref=ref, own=own, c0=c0, w=w: ref[pl.ds(own + at.start, at.size), pl.ds(c0, w)]]
            for k in range(1, g):
                parts.append(lambda at, b=recv, k=k: b[k - 1, at, :])
            _sum_rows(parts, acc, piece)
            state[li] = (acc, 0, w, piece, gbase + c * piece)

    ag_state = []
    for li, lane in enumerate(lanes):
        acc, _, w, length, gbase = state[li]
        i, c0 = lane[0], lane[1]
        if lane[4]:
            fulls[i][pl.ds(pl.multiple_of(gbase, 8), length), pl.ds(c0, w)] = acc[...]
        else:
            outs[i][...] = acc[...]
        ag_state.append((length, gbase))
    ag_base = []
    total = 0
    for lane in lanes:
        ag_base.append(total)
        total += sum(info(name)[0] - 1 for name in lane[4])
    for t in range(max(len(lane[4]) for lane in lanes)):
        pending = []
        offsets = [ag_base[li] + sum(info(n)[0] - 1 for n in lane[4][:t]) for li, lane in enumerate(lanes)]
        for li, lane in enumerate(lanes):
            if t >= len(lane[4]):
                continue
            g, c, peer = info(lane[4][t])
            length, gbase = ag_state[li]
            full = fulls[lane[0]]
            cols = pl.ds(lane[1], lane[2])
            mine = pl.ds(pl.multiple_of(gbase, 8), length)
            ai = offsets[li]
            for k in range(1, g):
                j = (c + k) % g
                cp = pltpu.make_async_remote_copy(
                    src_ref=full.at[mine, cols],
                    dst_ref=full.at[mine, cols],
                    send_sem=ag_send.at[ai + k - 1],
                    recv_sem=ag_recv.at[ai + g - k - 1],
                    device_id=peer(j),
                    device_id_type=mesh_id,
                )
                cp.start()
                sends.append(cp)
            pending.append(li)
        for li in pending:
            lane = lanes[li]
            g, c, peer = info(lane[4][t])
            length, gbase = ag_state[li]
            full = fulls[lane[0]]
            cols = pl.ds(lane[1], lane[2])
            ai = offsets[li]
            start = gbase - c * length
            for k in range(1, g):
                j = (c + k) % g
                theirs = pl.ds(pl.multiple_of(start + j * length, 8), length)
                pltpu.make_async_remote_copy(
                    src_ref=full.at[theirs, cols],
                    dst_ref=full.at[theirs, cols],
                    send_sem=ag_send.at[ai + k - 1],
                    recv_sem=ag_recv.at[ai + k - 1],
                    device_id=peer(j),
                    device_id_type=mesh_id,
                ).wait_recv()
            ag_state[li] = (length * g, start)
    gathered = sorted({lane[0] for lane in lanes if lane[4]})
    for i in gathered:
        outs[i][...] = fulls[i][...]
    for cp in sends:
        cp.wait_send()


def lane_reduce(inputs, lanes, collective_id):
    n_dom = lax.axis_size("dom")
    n_rep = lax.axis_size("rep")
    scratch = []
    recv_shapes, acc_shapes = [], []
    n_rs = n_ag = 0
    out_shapes = [None] * len(inputs)
    for i, c0, w, rs, ag in lanes:
        length = inputs[i].shape[0]
        recv, accs = [], []
        for name in rs:
            g = _stage(name, 0, 0, n_dom, n_rep)[0]
            piece = length // g
            recv.append(pltpu.VMEM((max(g - 1, 1), piece, w), jnp.float32))
            accs.append(pltpu.VMEM((piece, w), jnp.float32))
            length = piece
            n_rs += g - 1
        n_ag += sum(_stage(name, 0, 0, n_dom, n_rep)[0] - 1 for name in ag)
        scratch += recv + accs
        out_shapes[i] = inputs[i].shape if ag else (length, w)
    for i, x in enumerate(inputs):
        scratch.append(pltpu.VMEM(x.shape if any(l[0] == i and l[4] for l in lanes) else (8, 128), jnp.float32))
    scratch += [
        pltpu.SemaphoreType.DMA((max(1, n_rs),)),
        pltpu.SemaphoreType.DMA((max(1, n_rs),)),
        pltpu.SemaphoreType.DMA((max(1, n_ag),)),
        pltpu.SemaphoreType.DMA((max(1, n_ag),)),
    ]
    moved = sum(x.size for x in inputs) * 4
    return pl.pallas_call(
        functools.partial(_lane_kernel, tuple(lanes), (n_dom, n_rep), len(inputs)),
        out_shape=[jax.ShapeDtypeStruct(shape, jnp.float32) for shape in out_shapes],
        in_specs=[pl.BlockSpec(memory_space=pltpu.VMEM)] * len(inputs),
        out_specs=[pl.BlockSpec(memory_space=pltpu.VMEM)] * len(inputs),
        scratch_shapes=scratch,
        compiler_params=pltpu.CompilerParams(
            collective_id=collective_id, has_side_effects=True, vmem_limit_bytes=62 * 1024 * 1024
        ),
        cost_estimate=pl.CostEstimate(flops=moved, transcendentals=0, bytes_accessed=moved * 4),
    )(*inputs)


def pick_rows(table, ids):
    hot = (ids[:, None] == jnp.arange(table.shape[0], dtype=ids.dtype)[None, :]).astype(table.dtype)
    return jnp.dot(hot, table, preferred_element_type=jnp.float32).astype(table.dtype)


def local(entities, relations, head_local, rel_ids, tail_part, tail_local, neg_local):
    factor = 1.0 / math.sqrt(D)
    ent_dev = entities.shape[0]
    columns = entities.shape[1]
    edge_count = head_local.shape[0]
    part_count = lax.axis_size("dom")
    capacity = 2 * edge_count // part_count
    slot_count = part_count * capacity
    relation_count = relations.shape[0]
    head_rows = pick_rows(entities, head_local)
    selectors = [(rel_ids == relation)[:, None] for relation in range(relation_count)]
    query_sum = jnp.zeros((edge_count, columns), jnp.float32)
    for relation in range(relation_count):
        picked = jnp.where(selectors[relation], head_rows, jnp.zeros_like(head_rows))
        query_sum = query_sum + jnp.dot(
            picked, relations[relation], preferred_element_type=jnp.float32
        )
    queries = query_sum.astype(jnp.bfloat16)
    target = tail_part[:, 0]
    target_hot = (target[:, None] == jnp.arange(part_count, dtype=jnp.int32)[None, :]).astype(
        jnp.int32
    )
    earlier = jnp.cumsum(target_hot, axis=0) - target_hot
    position = jnp.sum(earlier * target_hot, axis=1)
    slot_index = target * capacity + position
    slot_match = (slot_index[None, :] == jnp.arange(slot_count, dtype=jnp.int32)[:, None]).astype(
        jnp.int32
    )
    filled = jnp.sum(slot_match, axis=1) > 0
    source = jnp.sum(slot_match * jnp.arange(edge_count, dtype=jnp.int32)[None, :], axis=1)
    send_ids = jnp.sum(slot_match * tail_local[None, :], axis=1).reshape(part_count, capacity)
    recv_ids = lax.all_to_all(send_ids, "dom", split_axis=0, concat_axis=0, tiled=True)
    looked_up = pick_rows(entities, recv_ids.reshape(-1)).reshape(
        part_count, capacity, columns
    )
    returned = lax.all_to_all(looked_up, "dom", split_axis=0, concat_axis=0, tiled=True)
    tail_embed = pick_rows(returned.reshape(slot_count, columns), slot_index)
    own_negs = pick_rows(entities, neg_local)
    negatives = lax.all_gather(own_negs, "dom", axis=0, tiled=True)
    positive = (
        jnp.sum(queries.astype(jnp.float32) * tail_embed.astype(jnp.float32), axis=1) * factor
    )
    scores = (
        lax.dot_general(
            queries, negatives, (((1,), (1,)), ((), ())), preferred_element_type=jnp.float32
        )
        * factor
    )
    row_max = jnp.maximum(positive, jnp.max(scores, axis=1))
    exp_pos = jnp.exp(positive - row_max)
    exp_neg = jnp.exp(scores - row_max[:, None])
    partition_sum = exp_pos + jnp.sum(exp_neg, axis=1)
    edge_loss = jnp.log(partition_sum) + row_max - positive
    prob_pos = exp_pos / partition_sum
    prob_neg = (exp_neg / partition_sum[:, None]).astype(jnp.bfloat16)
    mixed = jnp.dot(prob_neg, negatives, preferred_element_type=jnp.float32)
    query_grad = (
        factor * ((prob_pos - 1.0)[:, None] * tail_embed.astype(jnp.float32) + mixed)
    ).astype(jnp.bfloat16)
    tail_grad = factor * (prob_pos - 1.0)[:, None] * queries.astype(jnp.float32)
    head_grad = jnp.zeros((edge_count, columns), jnp.float32)
    rel_terms = []
    for relation in range(relation_count):
        picked_grad = jnp.where(selectors[relation], query_grad, jnp.zeros_like(query_grad))
        head_grad = head_grad + lax.dot_general(
            picked_grad,
            relations[relation],
            (((1,), (1,)), ((), ())),
            preferred_element_type=jnp.float32,
        )
        picked_rows = jnp.where(selectors[relation], head_rows, jnp.zeros_like(head_rows))
        rel_terms.append(
            lax.dot_general(
                picked_rows,
                query_grad,
                (((0,), (0,)), ((), ())),
                preferred_element_type=jnp.float32,
            )
        )
    rel_stack, prob_neg_late, queries_late = lax.optimization_barrier(
        (jnp.stack(rel_terms), prob_neg, queries)
    )
    neg_grad = factor * lax.dot_general(
        prob_neg_late, queries_late, (((0,), (0,)), ((), ())), preferred_element_type=jnp.float32
    )
    scale = factor * (prob_pos - 1.0)
    scale_hi = lax.reduce_precision(scale, exponent_bits=8, mantissa_bits=7)
    scale_rest = scale - scale_hi
    scale_mid = lax.reduce_precision(scale_rest, exponent_bits=8, mantissa_bits=7)
    scale_lo = scale_rest - scale_mid
    pack = jnp.concatenate(
        [
            queries,
            jnp.stack([scale_hi, scale_mid, scale_lo], axis=1).astype(jnp.bfloat16),
            jnp.zeros((edge_count, 125), jnp.bfloat16),
        ],
        axis=1,
    )
    pack_send = jnp.dot(
        slot_match.astype(jnp.bfloat16), pack, preferred_element_type=jnp.float32
    ).astype(jnp.bfloat16)
    pack_recv = lax.all_to_all(
        pack_send.reshape(part_count, capacity, pack.shape[1]),
        "dom",
        split_axis=0,
        concat_axis=0,
        tiled=True,
    ).reshape(slot_count, pack.shape[1])
    recv_scale = (
        pack_recv[:, columns].astype(jnp.float32) + pack_recv[:, columns + 1].astype(jnp.float32)
    ) + pack_recv[:, columns + 2].astype(jnp.float32)
    grad_recv = recv_scale[:, None] * pack_recv[:, :columns].astype(jnp.float32)
    rep_count = lax.axis_size("rep")
    neg_order = neg_grad.reshape(part_count // 8, 4, 2, rep_count, -1, columns)
    neg_order = neg_order.transpose(2, 3, 1, 0, 4, 5).reshape(-1, columns)
    orders = (("core", "x", "y", "z"), ("core", "y", "x", "z"))
    width = columns // len(orders)
    lanes = [(0, width * i, width, order, order[::-1]) for i, order in enumerate(orders)]
    lanes.append((1, 0, columns, ("core", "y", "x", "z"), ()))
    relation_flat, owned = lane_reduce([rel_stack.reshape(-1, columns), neg_order], lanes, 0)
    relation_grad = relation_flat.reshape(rel_stack.shape)
    neg_rows = owned.shape[0]
    neg_ids = lax.dynamic_slice_in_dim(neg_local, lax.axis_index("rep") * neg_rows, neg_rows)
    target_ids = jnp.concatenate([head_local, recv_ids.reshape(-1), neg_ids])
    target_rows = jnp.concatenate(
        [head_grad, grad_recv.reshape(slot_count, columns), owned], axis=0
    )
    block_rows = ent_dev
    block_count = ent_dev // block_rows

    rows_hi = lax.reduce_precision(target_rows, exponent_bits=8, mantissa_bits=7)
    rows_rest = target_rows - rows_hi
    rows_mid = lax.reduce_precision(rows_rest, exponent_bits=8, mantissa_bits=7)
    rows_split = jnp.concatenate([rows_hi, rows_mid, rows_rest - rows_mid], axis=1).astype(
        jnp.bfloat16
    )

    def add_block(start):
        hot = (
            target_ids[None, :] == (start + jnp.arange(block_rows, dtype=jnp.int32))[:, None]
        ).astype(jnp.bfloat16)
        parts = jnp.dot(hot, rows_split, preferred_element_type=jnp.float32)
        return (parts[:, :columns] + parts[:, columns : 2 * columns]) + parts[:, 2 * columns :]

    local_grad = lax.map(add_block, jnp.arange(block_count, dtype=jnp.int32) * block_rows).reshape(
        ent_dev, columns
    )
    entity_grad = tree_reduce(local_grad, ("y",), ("y",), 2)
    return (entity_grad, relation_grad, edge_loss)


def solution(mesh):
    return jax.shard_map(
        local,
        mesh=mesh,
        in_specs=(
            P("dom", None),
            P(),
            P(("dom", "rep")),
            P(("dom", "rep")),
            P(("dom", "rep"), None),
            P(("dom", "rep")),
            P("dom"),
        ),
        out_specs=(P("dom", None), P(), P(("dom", "rep"))),
        check_vma=False,
    )
```
